512 devices in a mesh: wide: 64 (over z, y), narrow: 8 (over x, core).
Axes of the slice: x: 4, y: 4, z: 16, core: 2. Of those that a mesh axis runs over, the one named last changes fastest.
Arguments:
- tracers: float32 [13, 16, 256, 1024], P(None, None, 'wide', 'narrow'), may hold values from -6 to 6
- courant_x: float32 [16, 256, 1024], P(None, 'wide', 'narrow'), may hold values from -0.24 to 0.24
- courant_y: float32 [16, 256, 1024], P(None, 'wide', 'narrow'), may hold values from -0.24 to 0.24
- physics_ref: float32 [13, 16], replicated, may hold values from -6 to 6
- class_coeffs: float32 [2, 3, 13], replicated, may hold values from 0.1 to 2
- span_target: int32 [256, 1024], P('wide', 'narrow'), may hold values from 0 to 32767, as said below
- cloud_class: int32 [256, 1024], P('wide', 'narrow'), may hold values from 0 to 2, as said below
Outputs:
- state_out: float32 [13, 16, 256, 1024], P(None, None, 'wide', 'narrow')
- span_diag: float32 [256, 1024], P('wide', 'narrow')
The draws below stay inside these ranges and needn't reach their ends.
Inputs may be any that keep to these rules, and one draw needn't show every extreme that they name: `span_target`: within each block of 128 grid columns held by one index of narrow, the values are a permutation of 0 .. 32767; v names slot v % 512 of span v // 512, and a device's cell of local index r * 128 + c has grid position (row block start + r, column block start + c), a slot likewise in span order. Each device sends exactly 2 cells to every other span of its column block; its other cells go to its own span. `cloud_class`: A cell's class is that of its slot: slots 0 .. 63 of every span are class 2, the next 128 slots class 1, the rest class 0.
All inputs are finite; a program needn't handle non-finite values.
Results may differ from the reference program's by a relative error of at most 0.0001.
Values sent between devices are 32-bit elements; how exact they have to be, the bound alone decides.
A program may use at most 64 MiB of HBM per device.

```python
import math
import jax
import jax.numpy as jnp

NF = 13
LEV = 16
R_DEV = 4
C_DEV = 128
DYN_STEPS = 2
CELLS = 512
CAP = 2
DEEP = 64
MID = 128
ROWS = 256
COLS = 1024
N_WIDE = 64
N_NARROW = 8


def layout_group(group_key):
    wide_count = N_WIDE
    incoming = (wide_count - 1) * CAP
    keys = jax.random.split(group_key, 4)
    richness = jax.random.randint(keys[0], (wide_count,), 0, 4)
    slots = jnp.arange(CELLS, dtype=jnp.int32)
    slot_class = jnp.where(slots < DEEP, 2, jnp.where(slots < DEEP + MID, 1, 0)).astype(jnp.int32)
    noise = jax.random.randint(keys[1], (wide_count, CELLS), 0, 4096)
    score = (noise + slot_class[None, :] * (3 - richness[:, None]) * 4096) * CELLS + slots[None, :]
    picked = jnp.argsort(-score, axis=1)
    chosen = picked[:, :incoming]
    kept = picked[:, incoming:]
    chosen_class = slot_class[chosen]
    chosen_noise = jnp.take_along_axis(noise, chosen, axis=1)
    second_key = (chosen_class * 4096 + chosen_noise) * CELLS + chosen
    chosen = jnp.take_along_axis(chosen, jnp.argsort(-second_key, axis=1), axis=1)
    devices = jnp.arange(wide_count, dtype=jnp.int32)
    source_noise = jax.random.randint(keys[2], (wide_count, wide_count), 0, 4096)
    source_key = (richness[None, :] * 4096 + source_noise) * wide_count + devices[None, :]
    source_key = jnp.where(devices[:, None] == devices[None, :], -1, source_key)
    source_order = jnp.argsort(-source_key, axis=1)
    source_rank = jnp.argsort(source_order, axis=1)
    cell_score = jax.random.randint(keys[3], (wide_count, CELLS), 0, 65536) * CELLS + slots[None, :]
    cell_perm = jnp.argsort(cell_score, axis=1)
    movers = cell_perm[:, :incoming].reshape(wide_count, wide_count - 1, CAP)
    stayers = cell_perm[:, incoming:]
    peer_rank = jnp.arange(wide_count - 1, dtype=jnp.int32)
    destination = peer_rank[None, :] + (peer_rank[None, :] >= devices[:, None]).astype(jnp.int32)
    sender_rank = source_rank[destination, devices[:, None]]
    position = sender_rank[:, :, None] * CAP + jnp.arange(CAP, dtype=jnp.int32)[None, None, :]
    dest_slot = chosen[destination[:, :, None], position]
    mover_value = destination[:, :, None] * CELLS + dest_slot
    stay_value = devices[:, None] * CELLS + kept
    sender_index = jnp.broadcast_to(devices[:, None, None], movers.shape)
    target = jnp.zeros((wide_count, CELLS), jnp.int32)
    target = target.at[sender_index, movers].set(mover_value)
    target = target.at[jnp.broadcast_to(devices[:, None], stayers.shape), stayers].set(stay_value)
    klass = slot_class[target % CELLS]
    return (target.astype(jnp.int32), klass.astype(jnp.int32))


def joint_layout(key):
    group_keys = jax.random.split(key, N_NARROW)
    targets, classes = jax.vmap(layout_group)(group_keys)

    def arrange(values):
        return values.reshape(N_NARROW, N_WIDE, R_DEV, C_DEV).transpose(1, 2, 0, 3).reshape(N_WIDE * R_DEV, N_NARROW * C_DEV)
    return (arrange(targets), arrange(classes))


def draw_span_target(key, part):
    return joint_layout(jax.random.fold_in(key, 11))[0]


def draw_cloud_class(key, part):
    return joint_layout(jax.random.fold_in(key, 11))[1]


def block_levels(own_key, shape, cuts, smallest, high):
    def one(axis_at, parts):
        draws = jax.random.uniform(jax.random.fold_in(jax.random.fold_in(own_key, 6), axis_at), (parts,), jnp.float32, smallest / len(cuts), high / len(cuts))
        return jnp.repeat(jnp.exp(draws), shape[axis_at] // parts).reshape((-1,) + (1,) * (len(shape) - axis_at - 1))

    level = one(*cuts[0])
    for cut in cuts[1:]:
        level = level * one(*cut)
    return level


def centred(stream_key, shape, spread, reach, cuts=(), kind=jnp.bfloat16):
    result = jax.random.normal(stream_key, shape, jnp.float32) * spread
    if len(cuts) > 0:
        result = block_levels(stream_key, shape, cuts, -0.22, 0.18) * result
    return jnp.clip(result, min=-reach, max=reach).astype(kind)


def setup_inputs(seed: int = 0) -> dict:
    streams_of = jax.random.split(jax.random.key(seed), 8)
    return {
        "tracers": centred(streams_of[0], (NF, LEV, ROWS, COLS), 1.0, 6.0, ((2, 64), (3, 8)), jnp.float32),
        "courant_x": jnp.clip(jax.random.uniform(streams_of[1], (LEV, ROWS, COLS), jnp.float32, -0.24, 0.24) * block_levels(streams_of[1], (LEV, ROWS, COLS), ((1, 64), (2, 8)), -0.4, 0.0), -0.24, 0.24),
        "courant_y": jnp.clip(jax.random.uniform(streams_of[2], (LEV, ROWS, COLS), jnp.float32, -0.24, 0.24) * block_levels(streams_of[2], (LEV, ROWS, COLS), ((1, 64), (2, 8)), -0.4, 0.0), -0.24, 0.24),
        "physics_ref": centred(streams_of[3], (NF, LEV), 1.0, 6.0, (), jnp.float32),
        "class_coeffs": jnp.clip(jnp.exp(jax.random.uniform(streams_of[4], (2, 3, NF), jnp.float32, math.log(0.1), math.log(2.0))), 0.1, 2.0),
        "span_target": draw_span_target(jax.random.fold_in(streams_of[7], 71), 0),
        "cloud_class": draw_cloud_class(jax.random.fold_in(streams_of[7], 71), 0),
    }


def solve_levels(right_side, diffusion, relax_rate):
    levels = right_side.shape[1]
    coupling = -diffusion
    middle = 1.0 + relax_rate + 2.0 * diffusion
    edge_diag = 1.0 + relax_rate + diffusion
    upper_ratio = [coupling / edge_diag]
    partial_value = [right_side[:, 0] / edge_diag]
    for level_index in range(1, levels):
        diagonal = edge_diag if level_index == levels - 1 else middle
        denominator = diagonal - coupling * upper_ratio[-1]
        upper_ratio.append(coupling / denominator)
        partial_value.append((right_side[:, level_index] - coupling * partial_value[-1]) / denominator)
    solved = [partial_value[-1]]
    for level_index in range(levels - 2, -1, -1):
        solved.append(partial_value[level_index] - upper_ratio[level_index] * solved[-1])
    return jnp.stack(solved[::-1], axis=1)


def column_physics(advected, klass, class_coeffs, physics_ref):
    fields = advected.shape[0]
    count = advected.shape[2]
    diff_sel = jnp.zeros((fields, count), jnp.float32)
    rate_sel = jnp.zeros((fields, count), jnp.float32)
    substeps = jnp.zeros((count,), jnp.float32)
    for category, repeats in ((0, 1.0), (1, 2.0), (2, 4.0)):
        picked = (klass == category).astype(jnp.float32)
        diff_sel = diff_sel + picked[None, :] * class_coeffs[0, category][:, None]
        rate_sel = rate_sel + picked[None, :] * class_coeffs[1, category][:, None]
        substeps = substeps + picked * repeats
    diffusion = diff_sel / substeps[None, :]
    relax_rate = rate_sel / substeps[None, :]
    state = advected
    for substep in range(4):
        solved = solve_levels(state + relax_rate[:, None, :] * physics_ref[:, :, None], diffusion, relax_rate)
        state = jnp.where(substeps[None, None, :] > substep, solved, state)
    return state - advected


def advect_once(tracers, courant_x, courant_y):
    east_cell = jnp.roll(tracers, -1, axis=3)
    north_cell = jnp.roll(tracers, -1, axis=2)
    flux_east = jnp.maximum(courant_x, 0.0) * tracers + jnp.minimum(courant_x, 0.0) * east_cell
    flux_north = jnp.maximum(courant_y, 0.0) * tracers + jnp.minimum(courant_y, 0.0) * north_cell
    return tracers - (flux_east - jnp.roll(flux_east, 1, axis=3)) - (flux_north - jnp.roll(flux_north, 1, axis=2))


def reference(tracers, courant_x, courant_y, physics_ref, class_coeffs, span_target, cloud_class):
    advected = tracers
    for step in range(DYN_STEPS):
        advected = advect_once(advected, courant_x, courant_y)
    fields, levels, rows_all, cols_all = tracers.shape
    flat = advected.reshape(fields, levels, rows_all * cols_all)
    tendency = column_physics(flat, cloud_class.reshape(-1), class_coeffs, physics_ref)
    state_out = (flat + tendency).reshape(tracers.shape)
    heat = jnp.mean(tendency * tendency, axis=(0, 1)).reshape(rows_all, cols_all)
    group_start = (jnp.arange(cols_all, dtype=jnp.int32) // C_DEV) * C_DEV
    dest_rows = (span_target // C_DEV).astype(jnp.int32)
    dest_cols = (group_start[None, :] + span_target % C_DEV).astype(jnp.int32)
    span_diag = jnp.zeros((rows_all, cols_all), jnp.float32).at[dest_rows, dest_cols].set(heat)
    return state_out, span_diag
```

```python
import functools

import jax
import jax.numpy as jnp
from jax import lax
from jax.experimental import pallas as pl
from jax.experimental.pallas import tpu as pltpu
from jax.sharding import PartitionSpec as P

F32 = jnp.float32
NF, LEV, RD, CD = 13, 16, 4, 128
FP = 16
CELLS = RD * CD
CHUNKS = ((0, 4), (4, 8), (8, 11), (11, 13))
NC = len(CHUNKS)
NY = 4
HIGH = lax.Precision.HIGHEST


def kernel(
    n_wide,
    n_narrow,
    x_hbm,
    cx_hbm,
    cy_hbm,
    ref_hbm,
    cc_hbm,
    tgt_hbm,
    cls_hbm,
    out_hbm,
    span_hbm,
    q0,
    q1,
    adv,
    ob,
    cxb,
    cyb,
    cys,
    refb,
    ccb,
    tgtb,
    clsb,
    halo_n,
    halo_s,
    col_tx0,
    col_rx0,
    col_tx1,
    col_rx1,
    coef,
    t_inv,
    t_b,
    t_c,
    hib,
    lob,
    heat8,
    msg,
    got,
    spanb,
    in_sem,
    small_sem,
    row_send,
    row_recv,
    cy_send,
    cy_recv,
    col_send,
    col_recv,
    msg_send,
    msg_recv,
    out_sem,
    span_sem,
    ladder_sem,
):
    nz = n_wide // NY
    w = lax.axis_index("wide")
    n = lax.axis_index("narrow")
    z, y = w // NY, w % NY

    def wide_at(dz, dy):
        return ((z + dz + nz) % nz) * NY + (y + dy) % NY

    north, south = (w + 1) % n_wide, (w + n_wide - 1) % n_wide
    east, west = (n + 1) % n_narrow, (n + n_narrow - 1) % n_narrow
    ladder = nz == 16

    barrier = pltpu.get_barrier_semaphore()

    def hello(**at):
        pl.semaphore_signal(barrier, 1, device_id=at, device_id_type=pl.DeviceIdType.MESH)

    hello(wide=north)
    hello(wide=south)
    hello(narrow=east)
    hello(narrow=west)
    hellos = 4
    if ladder:
        for dy in (1, 2, 3):
            hello(wide=wide_at(0, dy))
        for dz in (1, -1, 2, -2):
            hello(wide=wide_at(dz, 0))
        hellos += 7
    else:
        for i in range(1, n_wide):
            hello(wide=(w + i) % n_wide)
        hellos += n_wide - 1

    def fields(f0, f1):
        return pl.ds(f0 * LEV, (f1 - f0) * LEV)

    small = []

    def load(src, dst):
        c = pltpu.make_async_copy(src, dst, small_sem.at[len(small)])
        c.start()
        small.append(c)

    for r in range(RD):
        load(cx_hbm.at[:, r], cxb.at[r])
    loads = []
    for k, (f0, f1) in enumerate(CHUNKS):
        for r in range(RD):
            c = pltpu.make_async_copy(
                x_hbm.at[fields(f0, f1), r],
                q0.at[r, fields(f0, f1)],
                in_sem.at[k, r],
            )
            c.start()
            loads.append(c)
    for r in range(RD):
        load(cy_hbm.at[:, r], cyb.at[r])
    load(tgt_hbm, tgtb)
    load(cls_hbm, clsb)
    load(ref_hbm, refb.at[pl.ds(0, NF)])
    load(cc_hbm, ccb)

    lane = lax.broadcasted_iota(jnp.int32, (8, CD), 1)
    sub = lax.broadcasted_iota(jnp.int32, (8, CD), 0)
    first, last = lane == 0, lane == CD - 1
    edge = first | last
    even = lane % 2 == 0
    zero = jnp.zeros((8, CD), F32)
    refb[NF:FP, :] = jnp.zeros((FP - NF, LEV), F32)
    adv[:, NF * LEV : FP * LEV, :] = jnp.zeros((RD, (FP - NF) * LEV, CD), F32)

    def packed_field(piece, place):
        total = zero
        for h in range(2):
            for r in range(RD):
                e = jnp.where(edge, piece(r, h), 0.0)
                shift = 2 * (h * RD + r)
                total = total + (pltpu.roll(e, shift, 1) if shift else e)
        return pltpu.roll(total, place * 16, 1)

    def halves(h, f=None):
        return pl.ds(h * 8, 8) if f is None else pl.ds(pl.multiple_of(f * LEV + h * 8, 8), 8)

    for c in small[:RD]:
        c.wait()
    for c in loads:
        c.wait()

    def pack0(f, total):
        return total + packed_field(lambda r, h: q0[r, halves(h, f), :], f % 8)

    col_tx0[0] = lax.fori_loop(0, 8, pack0, zero)
    rest = lax.fori_loop(8, NF, pack0, zero)
    col_tx0[1] = rest + packed_field(lambda r, h: cxb[r, halves(h), :], NF % 8)
    for c in small[RD:]:
        c.wait()

    pl.semaphore_wait(barrier, hellos)

    sends = []

    def send(src, dst, ssem, rsem, **at):
        c = pltpu.make_async_remote_copy(
            src, dst, ssem, rsem, device_id=at, device_id_type=pl.DeviceIdType.MESH
        )
        c.start()
        sends.append(c)
        return c

    if ladder:
        for dz in (1, -1):
            pl.semaphore_signal(
                ladder_sem.at[0],
                1,
                device_id={"wide": wide_at(dz, 0)},
                device_id_type=pl.DeviceIdType.MESH,
            )

    col0 = (
        send(col_tx0, col_rx0.at[0], col_send.at[0, 0], col_recv.at[0, 0], narrow=east),
        send(col_tx0, col_rx0.at[1], col_send.at[0, 1], col_recv.at[0, 1], narrow=west),
    )
    cy_copy = send(cyb.at[RD - 1], cys, cy_send, cy_recv, wide=north)

    def send_rows(step, k, q):
        f0, f1 = CHUNKS[k]
        part = fields(f0, f1)
        up = send(
            q.at[RD - 1, part],
            halo_s.at[step, part],
            row_send.at[step, k, 0],
            row_recv.at[step, k, 0],
            wide=north,
        )
        down = send(
            q.at[0, part],
            halo_n.at[step, part],
            row_send.at[step, k, 1],
            row_recv.at[step, k, 1],
            wide=south,
        )
        return (up, down)

    rows0 = [send_rows(0, k, q0) for k in range(NC)]

    fsub = lax.broadcasted_iota(jnp.int32, (FP, NF), 0)
    flane = lax.broadcasted_iota(jnp.int32, (FP, NF), 1)
    by_class = []
    for k in range(3):
        pair = []
        for j in range(2):
            row = jnp.broadcast_to(ccb[k, j : j + 1, :], (FP, NF))
            column = jnp.sum(jnp.where(fsub == flane, row, 0.0), axis=1, keepdims=True)
            column = column / float((1, 2, 4)[k])
            pair.append([jnp.broadcast_to(column[g * 8 : g * 8 + 8], (8, CD)) for g in range(2)])
        by_class.append(pair)

    def class_row(r):
        return jnp.broadcast_to(clsb[pl.ds(r, 1), :], (8, CD))

    for g in range(2):
        refs = refb[g * 8 : g * 8 + 8, :]

        def tables(r, carry, g=g, refs=refs):
            kind = class_row(r)
            pick = lambda j: jnp.where(
                kind == 2,
                by_class[2][j][g],
                jnp.where(kind == 1, by_class[1][j][g], by_class[0][j][g]),
            )
            d, rate = pick(0), pick(1)
            middle = 1.0 + rate + 2.0 * d
            outer = 1.0 + rate + d
            ratio = None
            for l in range(LEV):
                diagonal = outer if l in (0, LEV - 1) else middle
                denominator = diagonal if ratio is None else diagonal - d * ratio
                inverse = 1.0 / denominator
                ratio = d * inverse
                t_inv[r, g, l] = inverse
                t_c[r, g, l] = ratio
                t_b[r, g, l] = rate * jnp.broadcast_to(refs[:, l : l + 1], (8, CD)) * inverse
            return carry

        lax.fori_loop(0, RD, tables, 0)

    target_f = tgtb[...].astype(F32)
    t_rows = [jnp.broadcast_to(target_f[r : r + 1], (8, CD)) for r in range(RD)]
    o_rows = [jnp.broadcast_to(tgtb[r : r + 1, :] // CELLS, (8, CD)) for r in range(RD)]

    def ends(t, carry):
        d = t * 8 + sub
        hi = jnp.full((8, CD), -1.0, F32)
        lo = jnp.full((8, CD), 1e9, F32)
        for r in range(RD):
            hit = o_rows[r] == d
            hi = jnp.maximum(hi, jnp.where(hit, t_rows[r], -1.0))
            lo = jnp.minimum(lo, jnp.where(hit, t_rows[r], 1e9))
        hib[t] = jnp.broadcast_to(jnp.max(hi, axis=1, keepdims=True), (8, CD))
        lob[t] = jnp.broadcast_to(jnp.min(lo, axis=1, keepdims=True), (8, CD))
        return carry

    lax.fori_loop(0, n_wide // 8, ends, 0)

    def merged(from_west, from_east):
        return jnp.where(even, pltpu.roll(from_west, 1, 1), pltpu.roll(from_east, CD - 1, 1))

    col0[0].wait_recv()
    col0[1].wait_recv()
    edges0 = [merged(col_rx0[0, i], col_rx0[1, i]) for i in range(2)]
    cy_copy.wait_recv()
    cx_edges = pltpu.roll(edges0[1], CD - 16 * (NF % 8), 1)
    for h in range(2):
        for r in range(RD):
            shift = 2 * (h * RD + r)
            here_x = cxb[r, halves(h), :]
            got_x = pltpu.roll(cx_edges, CD - shift, 1) if shift else cx_edges
            west_x = jnp.where(first, got_x, pltpu.roll(here_x, 1, 1))
            here_y = cyb[r, halves(h), :]
            south_y = cyb[r - 1, halves(h), :] if r else cys[halves(h), :]
            at = (r, halves(h), slice(None))
            coef[(0,) + at] = (
                1.0
                - jnp.maximum(here_x, 0.0)
                + jnp.minimum(west_x, 0.0)
                - jnp.maximum(here_y, 0.0)
                + jnp.minimum(south_y, 0.0)
            )
            coef[(1,) + at] = -jnp.minimum(here_x, 0.0)
            coef[(2,) + at] = jnp.maximum(west_x, 0.0)
            coef[(3,) + at] = -jnp.minimum(here_y, 0.0)
            coef[(4,) + at] = jnp.maximum(south_y, 0.0)

    def transport(step, k, src, dst, edges, pack):
        def field(f, total):
            mine = pltpu.roll(edges, (CD - 16 * (f % 8)) % CD, 1)
            new = {}
            for h in range(2):
                part, rows = halves(h), halves(h, f)
                q = [src[r, rows, :] for r in range(RD)]
                q = [halo_s[step, rows, :]] + q + [halo_n[step, rows, :]]
                for r in range(RD):
                    here = q[r + 1]
                    shift = 2 * (h * RD + r)
                    around = pltpu.roll(mine, CD - shift, 1) if shift else mine
                    to_east = jnp.where(last, around, pltpu.roll(here, CD - 1, 1))
                    to_west = jnp.where(first, around, pltpu.roll(here, 1, 1))
                    v = (
                        (coef[0, r, part, :] * here + coef[1, r, part, :] * to_east)
                        + (coef[3, r, part, :] * q[r + 2] + coef[4, r, part, :] * q[r])
                        + coef[2, r, part, :] * to_west
                    )
                    dst[r, rows, :] = v
                    new[r, h] = v
            if pack:
                total = total + packed_field(lambda r, h: new[r, h], f % 8)
            return total

        f0, f1 = CHUNKS[k]
        return lax.fori_loop(f0, f1, field, zero)

    def rung(i, dz):
        if ladder:
            pl.semaphore_wait(ladder_sem.at[i], 2)
            if dz:
                for s in (dz, -dz):
                    pl.semaphore_signal(
                        ladder_sem.at[i + 1],
                        1,
                        device_id={"wide": wide_at(s, 0)},
                        device_id_type=pl.DeviceIdType.MESH,
                    )

    rows1, cols1 = [], []
    for k in range(NC):
        for c in rows0[k]:
            c.wait_recv()
        col_tx1[k] = transport(0, k, q0, q1, edges0[CHUNKS[k][0] // 8], True)
        rows1.append(send_rows(1, k, q1))
        cols1.append(
            (
                send(
                    col_tx1.at[k],
                    col_rx1.at[k, 0],
                    col_send.at[1 + k, 0],
                    col_recv.at[1 + k, 0],
                    narrow=east,
                ),
                send(
                    col_tx1.at[k],
                    col_rx1.at[k, 1],
                    col_send.at[1 + k, 1],
                    col_recv.at[1 + k, 1],
                    narrow=west,
                ),
            )
        )
        if k == 0:
            rung(0, 3)

    for r in range(RD):
        heat8[r] = zero

    def physics(g):
        def row(r, carry):
            kind = class_row(r)
            base = g * 8 * LEV
            start = [adv[r, pl.ds(base + l, 8, stride=LEV), :] for l in range(LEV)]
            state = list(start)
            for s in range(4):
                part = []
                for l in range(LEV):
                    v = state[l] * t_inv[r, g, l] + t_b[r, g, l]
                    if l:
                        v = v + t_c[r, g, l] * part[-1]
                    part.append(v)
                solved = [None] * LEV
                solved[LEV - 1] = part[LEV - 1]
                for l in range(LEV - 2, -1, -1):
                    solved[l] = part[l] + t_c[r, g, l] * solved[l + 1]
                if s == 0:
                    state = solved
                else:
                    keep = kind >= (1 if s == 1 else 2)
                    state = [jnp.where(keep, a, b) for a, b in zip(solved, state)]
            heat = zero
            for l in range(LEV):
                tendency = state[l] - start[l]
                heat = heat + tendency * tendency
                ob[r, pl.ds(base + l, 8, stride=LEV), :] = start[l] + tendency
            heat8[r] = heat8[r] + heat
            return carry

        lax.fori_loop(0, RD, row, 0)
        f0, f1 = g * 8, min(g * 8 + 8, NF)
        copies = []
        for r in range(RD):
            c = pltpu.make_async_copy(
                ob.at[r, fields(f0, f1)],
                out_hbm.at[fields(f0, f1), r],
                out_sem.at[g, r],
            )
            c.start()
            copies.append(c)
        return copies

    outs = []
    for k in range(NC):
        for c in rows1[k] + cols1[k]:
            c.wait_recv()
        transport(1, k, q1, adv, merged(col_rx1[k, 0], col_rx1[k, 1]), False)
        if k == 0:
            rung(1, 4)
        if CHUNKS[k][1] == 8:
            outs += physics(0)
    outs += physics(1)

    heats = []
    for r in range(RD):
        heat = jnp.sum(heat8[r], axis=0, keepdims=True) * (1.0 / (NF * LEV))
        heats.append(jnp.broadcast_to(heat, (8, CD)))
    for t in range(n_wide // 8):
        hi, lo = zero, zero
        for r in range(RD):
            hi = hi + jnp.where(t_rows[r] == hib[t], heats[r], 0.0)
            lo = lo + jnp.where(t_rows[r] == lob[t], heats[r], 0.0)
        hi = jnp.broadcast_to(jnp.sum(hi, axis=1, keepdims=True), (8, CD))
        lo = jnp.broadcast_to(jnp.sum(lo, axis=1, keepdims=True), (8, CD))
        msg[t * 8 : t * 8 + 8, :] = jnp.where(
            lane == 0, hi, jnp.where(lane == 1, lo, jnp.where(lane == 2, hib[t], lob[t]))
        )
    got[pl.ds(w, 1), :] = jnp.full((1, CD), -1.0, F32)

    rung(2, 0)

    def post(i, carry):
        m, dy = i // NY, i % NY
        dz = nz // 2 + (1 - 2 * (m % 2)) * ((m + 1) // 2)
        to = wide_at(dz, dy)
        pltpu.make_async_remote_copy(
            msg.at[pl.ds(to, 1)],
            got.at[pl.ds(w, 1)],
            msg_send,
            msg_recv,
            device_id={"wide": to},
            device_id_type=pl.DeviceIdType.MESH,
        ).start()
        return carry

    lax.fori_loop(0, n_wide - NY, post, 0)
    lax.fori_loop(n_wide - NY + 1, n_wide, post, 0)

    base = w * RD
    mine = zero
    wide_lane = lax.broadcasted_iota(jnp.int32, (CD, CD), 0)
    for r in range(RD):
        t_row = tgtb[r : r + 1, :]
        here = jnp.broadcast_to(t_row // CD - base, (8, CD))
        a = jnp.where((here == sub) & (sub < RD), heats[r], 0.0)
        b = jnp.where(jnp.broadcast_to(t_row % CD, (CD, CD)) == wide_lane, 1.0, 0.0)
        mine = mine + lax.dot_general(
            a, b, (((1,), (1,)), ((), ())), precision=HIGH, preferred_element_type=F32
        )

    for c in outs:
        c.wait()
    for c in sends:
        c.wait_send()

    everyone = pl.ds(0, n_wide - 1)
    pltpu.make_async_copy(msg.at[everyone], got.at[everyone], msg_recv).wait()
    rows = [zero for r in range(RD)]
    place = (w * CELLS + lane).astype(F32)
    for t in range(n_wide // 8):
        tile = got[t * 8 : t * 8 + 8, :]
        value = [jnp.broadcast_to(tile[:, i : i + 1], (8, CD)) for i in range(2)]
        slot = [jnp.broadcast_to(tile[:, i + 2 : i + 3], (8, CD)) for i in range(2)]
        for r in range(RD):
            for i in range(2):
                hit = slot[i] == place + float(r * CD)
                rows[r] = rows[r] + jnp.where(hit, value[i], 0.0)
    total = mine
    for r in range(RD):
        arrived = jnp.broadcast_to(jnp.sum(rows[r], axis=0, keepdims=True), (8, CD))
        total = total + jnp.where(sub == r, arrived, 0.0)
    spanb[...] = total[0:RD]
    c = pltpu.make_async_copy(spanb, span_hbm, span_sem)
    c.start()
    pltpu.make_async_copy(msg.at[everyone], got.at[everyone], msg_send).wait()
    c.wait()


def body(n_wide, n_narrow, tracers, courant_x, courant_y, physics_ref, class_coeffs, span_target, cloud_class):
    anyspace = pl.BlockSpec(memory_space=pl.ANY)
    dma, regular = pltpu.SemaphoreType.DMA, pltpu.SemaphoreType.REGULAR
    vm = lambda *shape: pltpu.VMEM(shape, F32)
    tiles = n_wide // 8
    state, span = pl.pallas_call(
        functools.partial(kernel, n_wide, n_narrow),
        out_shape=(
            jax.ShapeDtypeStruct((NF * LEV, RD, CD), F32),
            jax.ShapeDtypeStruct((RD, CD), F32),
        ),
        in_specs=[anyspace] * 7,
        out_specs=(anyspace, anyspace),
        scratch_shapes=[
            vm(RD, NF * LEV, CD),
            vm(RD, NF * LEV, CD),
            vm(RD, FP * LEV, CD),
            vm(RD, FP * LEV, CD),
            vm(RD, LEV, CD),
            vm(RD, LEV, CD),
            vm(LEV, CD),
            vm(FP, LEV),
            vm(3, 2, NF),
            pltpu.VMEM((RD, CD), jnp.int32),
            pltpu.VMEM((RD, CD), jnp.int32),
            vm(2, NF * LEV, CD),
            vm(2, NF * LEV, CD),
            vm(2, 8, CD),
            vm(2, 2, 8, CD),
            vm(NC, 8, CD),
            vm(NC, 2, 8, CD),
            vm(5, RD, LEV, CD),
            vm(RD, 2, LEV, 8, CD),
            vm(RD, 2, LEV, 8, CD),
            vm(RD, 2, LEV, 8, CD),
            vm(tiles, 8, CD),
            vm(tiles, 8, CD),
            vm(RD, 8, CD),
            vm(n_wide, CD),
            vm(n_wide, CD),
            vm(RD, CD),
            dma((NC, RD)),
            dma((12,)),
            dma((2, NC, 2)),
            dma((2, NC, 2)),
            dma,
            dma,
            dma((1 + NC, 2)),
            dma((1 + NC, 2)),
            dma,
            dma,
            dma((2, RD)),
            dma,
            regular((3,)),
        ],
        compiler_params=pltpu.CompilerParams(collective_id=0, has_side_effects=True),
        name="transport_physics",
    )(
        tracers.reshape(NF * LEV, RD, CD),
        courant_x,
        courant_y,
        physics_ref,
        jnp.transpose(class_coeffs, (1, 0, 2)),
        span_target,
        cloud_class,
    )
    return state.reshape(NF, LEV, RD, CD), span


def solution(mesh):
    return jax.shard_map(
        functools.partial(body, mesh.shape["wide"], mesh.shape["narrow"]),
        mesh=mesh,
        in_specs=(
            P(None, None, "wide", "narrow"),
            P(None, "wide", "narrow"),
            P(None, "wide", "narrow"),
            P(),
            P(),
            P("wide", "narrow"),
            P("wide", "narrow"),
        ),
        out_specs=(P(None, None, "wide", "narrow"), P("wide", "narrow")),
        check_vma=False,
    )
```

```python
import functools

import jax
import jax.numpy as jnp
from jax import lax
from jax.experimental import pallas as pl
from jax.experimental.pallas import tpu as pltpu
from jax.sharding import PartitionSpec as P

F32 = jnp.float32
NF, LEV, RD, CD = 13, 16, 4, 128
FP = 16
CELLS = RD * CD
HALF = LEV // 2
CHUNKS = ((0, 4), (4, 8), (8, 11), (11, 13))
NC = len(CHUNKS)
NY = 4
HIGH = lax.Precision.HIGHEST


def kernel(
    n_wide,
    n_narrow,
    x_hbm,
    cx_hbm,
    cy_hbm,
    ref_hbm,
    cc_hbm,
    tgt_hbm,
    cls_hbm,
    ob,
    got_out,
    mine_out,
    q0,
    q1,
    adv,
    cxb,
    cyb,
    cys,
    refb,
    ccb,
    tgtb,
    clsb,
    halo_n,
    halo_s,
    col_tx0,
    col_rx0,
    col_tx1,
    col_rx1,
    coef,
    t_inv,
    t_b,
    t_c,
    hib,
    lob,
    heat8,
    msg,
    got,
    in_sem,
    small_sem,
    row_send,
    row_recv,
    cy_send,
    cy_recv,
    col_send,
    col_recv,
    msg_send,
    msg_recv,
    ladder_sem,
):
    nz = n_wide // NY
    w = lax.axis_index("wide")
    n = lax.axis_index("narrow")
    z, y = w // NY, w % NY

    def wide_at(dz, dy):
        return ((z + dz + nz) % nz) * NY + (y + dy) % NY

    north, south = (w + 1) % n_wide, (w + n_wide - 1) % n_wide
    east, west = (n + 1) % n_narrow, (n + n_narrow - 1) % n_narrow
    ladder = nz == 16

    barrier = pltpu.get_barrier_semaphore()

    def hello(**at):
        pl.semaphore_signal(barrier, 1, device_id=at, device_id_type=pl.DeviceIdType.MESH)

    hello(wide=north)
    hello(wide=south)
    hello(narrow=east)
    hello(narrow=west)
    hellos = 4
    if ladder:
        for dy in (1, 2, 3):
            hello(wide=wide_at(0, dy))
        for dz in (1, -1, 2, -2):
            hello(wide=wide_at(dz, 0))
        hellos += 7
    else:
        for i in range(1, n_wide):
            hello(wide=(w + i) % n_wide)
        hellos += n_wide - 1

    def fields(f0, f1):
        return pl.ds(f0 * LEV, (f1 - f0) * LEV)

    small = []

    def load(src, dst):
        c = pltpu.make_async_copy(src, dst, small_sem.at[len(small)])
        c.start()
        small.append(c)

    for r in range(RD):
        load(cx_hbm.at[:, r], cxb.at[r])
    loads = []
    for k, (f0, f1) in enumerate(CHUNKS):
        for r in range(RD):
            c = pltpu.make_async_copy(
                x_hbm.at[fields(f0, f1), r],
                q0.at[r, fields(f0, f1)],
                in_sem.at[k, r],
            )
            c.start()
            loads.append(c)
    for r in range(RD):
        load(cy_hbm.at[:, r], cyb.at[r])
    load(tgt_hbm, tgtb)
    load(cls_hbm, clsb)
    load(ref_hbm, refb.at[pl.ds(0, NF)])
    load(cc_hbm, ccb)

    lane = lax.broadcasted_iota(jnp.int32, (8, CD), 1)
    sub = lax.broadcasted_iota(jnp.int32, (8, CD), 0)
    first, last = lane == 0, lane == CD - 1
    edge = first | last
    even = lane % 2 == 0
    zero = jnp.zeros((8, CD), F32)
    refb[NF:FP, :] = jnp.zeros((FP - NF, LEV), F32)
    adv[:, NF * LEV : FP * LEV, :] = jnp.zeros((RD, (FP - NF) * LEV, CD), F32)

    def spin(v, shift):
        shift %= CD
        return pltpu.roll(v, shift, 1) if shift else v

    def shift_of(r, f, h):
        return 2 * ((f % 8) * 8 + h * RD + r)

    def packed(v, r, f, h):
        return spin(jnp.where(edge, v, 0.0), shift_of(r, f, h))

    def halves(h, f=0):
        return pl.ds(f * LEV + h * 8, 8)

    for c in small[:RD]:
        c.wait()
    for c in loads:
        c.wait()

    for i in range(2):
        totals = []
        for r in range(RD):
            total = zero
            for f in range(8 * i, min(8 * i + 8, NF)):
                for h in range(2):
                    total = total + packed(q0[r, halves(h, f), :], r, f, h)
            if i:
                for h in range(2):
                    total = total + packed(cxb[r, halves(h), :], r, NF, h)
            totals.append(total)
        col_tx0[i] = (totals[0] + totals[1]) + (totals[2] + totals[3])
    for c in small[RD:]:
        c.wait()

    pl.semaphore_wait(barrier, hellos)

    sends = []

    def send(src, dst, ssem, rsem, **at):
        c = pltpu.make_async_remote_copy(
            src, dst, ssem, rsem, device_id=at, device_id_type=pl.DeviceIdType.MESH
        )
        c.start()
        sends.append(c)
        return c

    if ladder:
        for dz in (1, -1):
            pl.semaphore_signal(
                ladder_sem.at[0],
                1,
                device_id={"wide": wide_at(dz, 0)},
                device_id_type=pl.DeviceIdType.MESH,
            )

    col0 = (
        send(col_tx0, col_rx0.at[0], col_send.at[0, 0], col_recv.at[0, 0], narrow=east),
        send(col_tx0, col_rx0.at[1], col_send.at[0, 1], col_recv.at[0, 1], narrow=west),
    )
    cy_copy = send(cyb.at[RD - 1], cys, cy_send, cy_recv, wide=north)

    def send_rows(step, k, q):
        f0, f1 = CHUNKS[k]
        part = fields(f0, f1)
        up = send(
            q.at[RD - 1, part],
            halo_s.at[step, part],
            row_send.at[step, k, 0],
            row_recv.at[step, k, 0],
            wide=north,
        )
        down = send(
            q.at[0, part],
            halo_n.at[step, part],
            row_send.at[step, k, 1],
            row_recv.at[step, k, 1],
            wide=south,
        )
        return (up, down)

    rows0 = [send_rows(0, k, q0) for k in range(NC)]

    fsub = lax.broadcasted_iota(jnp.int32, (FP, NF), 0)
    flane = lax.broadcasted_iota(jnp.int32, (FP, NF), 1)
    by_class = []
    for k in range(3):
        pair = []
        for j in range(2):
            row = jnp.broadcast_to(ccb[k, j : j + 1, :], (FP, NF))
            column = jnp.sum(jnp.where(fsub == flane, row, 0.0), axis=1, keepdims=True)
            column = column / float((1, 2, 4)[k])
            pair.append([jnp.broadcast_to(column[g * 8 : g * 8 + 8], (8, CD)) for g in range(2)])
        by_class.append(pair)

    def class_row(r):
        return jnp.broadcast_to(clsb[pl.ds(r, 1), :], (8, CD))

    for g in range(2):
        refs = refb[g * 8 : g * 8 + 8, :]

        def tables(r, carry, g=g, refs=refs):
            kind = class_row(r)
            pick = lambda j: jnp.where(
                kind == 2,
                by_class[2][j][g],
                jnp.where(kind == 1, by_class[1][j][g], by_class[0][j][g]),
            )
            d, rate = pick(0), pick(1)
            middle = 1.0 + rate + 2.0 * d
            ratio = None
            for l in range(HALF):
                diagonal = middle if l else 1.0 + rate + d
                denominator = diagonal - d * ratio if l else diagonal
                level = [jnp.broadcast_to(refs[:, m : m + 1], (8, CD)) for m in (l, LEV - 1 - l)]
                even_ref, odd_ref = rate * (level[0] + level[1]), rate * (level[0] - level[1])
                if l < HALF - 1:
                    inverse = 1.0 / denominator
                    ratio = d * inverse
                    t_inv[r, g, l] = inverse
                    t_c[r, g, l] = ratio
                    t_b[r, g, l] = even_ref * inverse
                    t_b[r, g, HALF + l] = odd_ref * inverse
                else:
                    even_inv, odd_inv = 1.0 / (denominator - d), 1.0 / (denominator + d)
                    t_inv[r, g, l] = even_inv
                    t_inv[r, g, l + 1] = odd_inv
                    t_c[r, g, l] = d * even_inv
                    t_c[r, g, l + 1] = d * odd_inv
                    t_b[r, g, l] = even_ref * even_inv
                    t_b[r, g, HALF + l] = odd_ref * odd_inv
            return carry

        lax.fori_loop(0, RD, tables, 0)

    target_f = tgtb[...].astype(F32)
    t_rows = [jnp.broadcast_to(target_f[r : r + 1], (8, CD)) for r in range(RD)]
    o_rows = [jnp.broadcast_to(tgtb[r : r + 1, :] // CELLS, (8, CD)) for r in range(RD)]

    def ends(t, carry):
        d = t * 8 + sub
        hi = jnp.full((8, CD), -1.0, F32)
        lo = jnp.full((8, CD), 1e9, F32)
        for r in range(RD):
            hit = o_rows[r] == d
            hi = jnp.maximum(hi, jnp.where(hit, t_rows[r], -1.0))
            lo = jnp.minimum(lo, jnp.where(hit, t_rows[r], 1e9))
        hib[t] = jnp.broadcast_to(jnp.max(hi, axis=1, keepdims=True), (8, CD))
        lob[t] = jnp.broadcast_to(jnp.min(lo, axis=1, keepdims=True), (8, CD))
        return carry

    lax.fori_loop(0, n_wide // 8, ends, 0)

    def merged(from_west, from_east):
        return jnp.where(even, pltpu.roll(from_west, 1, 1), pltpu.roll(from_east, CD - 1, 1))

    col0[0].wait_recv()
    col0[1].wait_recv()
    edges0 = [merged(col_rx0[0, i], col_rx0[1, i]) for i in range(2)]
    cy_copy.wait_recv()
    for h in range(2):
        for r in range(RD):
            here_x = cxb[r, halves(h), :]
            got_x = spin(edges0[1], -shift_of(r, NF, h))
            west_x = jnp.where(first, got_x, pltpu.roll(here_x, 1, 1))
            here_y = cyb[r, halves(h), :]
            south_y = cyb[r - 1, halves(h), :] if r else cys[halves(h), :]
            at = (r, halves(h), slice(None))
            coef[(0,) + at] = (
                1.0
                - jnp.maximum(here_x, 0.0)
                + jnp.minimum(west_x, 0.0)
                - jnp.maximum(here_y, 0.0)
                + jnp.minimum(south_y, 0.0)
            )
            coef[(1,) + at] = -jnp.minimum(here_x, 0.0)
            coef[(2,) + at] = jnp.maximum(west_x, 0.0)
            coef[(3,) + at] = -jnp.minimum(here_y, 0.0)
            coef[(4,) + at] = jnp.maximum(south_y, 0.0)

    def transport(step, k, src, dst, edges, pack):
        f0, f1 = CHUNKS[k]
        total = [zero, zero]
        for h in range(2):
            part = halves(h)
            for r in range(RD):
                c = [coef[i, r, part, :] for i in range(5)]
                for f in range(f0, f1):
                    rows = halves(h, f)
                    here = src[r, rows, :]
                    north_q = src[r + 1, rows, :] if r < RD - 1 else halo_n[step, rows, :]
                    south_q = src[r - 1, rows, :] if r else halo_s[step, rows, :]
                    around = spin(edges, -shift_of(r, f, h))
                    east_q = jnp.where(last, around, spin(here, -1))
                    west_q = jnp.where(first, around, spin(here, 1))
                    v = ((c[0] * here + c[3] * north_q) + c[4] * south_q) + (
                        c[1] * east_q + c[2] * west_q
                    )
                    dst[r, rows, :] = v
                    if pack:
                        total[f % 2] = total[f % 2] + packed(v, r, f, h)
        return total[0] + total[1]

    def rung(i, dz):
        if ladder:
            pl.semaphore_wait(ladder_sem.at[i], 2)
            if dz:
                for s in (dz, -dz):
                    pl.semaphore_signal(
                        ladder_sem.at[i + 1],
                        1,
                        device_id={"wide": wide_at(s, 0)},
                        device_id_type=pl.DeviceIdType.MESH,
                    )

    rows1, cols1 = [], []
    for k in range(NC):
        for c in rows0[k]:
            c.wait_recv()
        col_tx1[k] = transport(0, k, q0, q1, edges0[CHUNKS[k][0] // 8], True)
        rows1.append(send_rows(1, k, q1))
        cols1.append(
            (
                send(
                    col_tx1.at[k],
                    col_rx1.at[k, 0],
                    col_send.at[1 + k, 0],
                    col_recv.at[1 + k, 0],
                    narrow=east,
                ),
                send(
                    col_tx1.at[k],
                    col_rx1.at[k, 1],
                    col_send.at[1 + k, 1],
                    col_recv.at[1 + k, 1],
                    narrow=west,
                ),
            )
        )
        if k == 0:
            rung(0, 3)

    for r in range(RD):
        heat8[r] = zero

    def physics(g):
        def at(l):
            return pl.ds(g * 8 * LEV + l, 8, stride=LEV)

        def pair(i, carry):
            rows = [2 * i, 2 * i + 1]
            kinds = [class_row(r) for r in rows]
            begin = []
            for r in rows:
                low = [adv[r, at(l), :] for l in range(HALF)]
                high = [adv[r, at(LEV - 1 - l), :] for l in range(HALF)]
                begin.append([a + b for a, b in zip(low, high)] + [a - b for a, b in zip(low, high)])
            state = [list(b) for b in begin]
            for s in range(4):
                part = [[None] * LEV for r in rows]
                for l in range(HALF):
                    for j, r in enumerate(rows):
                        for odd in range(2):
                            m = odd * HALF + l
                            v = state[j][m] * t_inv[r, g, l + (odd if l == HALF - 1 else 0)]
                            v = v + t_b[r, g, m]
                            if l:
                                own = l + (odd if l == HALF - 1 else 0)
                                v = v + t_c[r, g, own] * part[j][m - 1]
                            part[j][m] = v
                for l in range(HALF - 2, -1, -1):
                    for j, r in enumerate(rows):
                        for odd in range(2):
                            m = odd * HALF + l
                            part[j][m] = part[j][m] + t_c[r, g, l] * part[j][m + 1]
                for j in range(2):
                    if s:
                        keep = kinds[j] >= (1 if s == 1 else 2)
                        part[j] = [jnp.where(keep, a, b) for a, b in zip(part[j], state[j])]
                    state[j] = part[j]
            for j, r in enumerate(rows):
                heat = zero
                for l in range(HALF):
                    even_t = 0.5 * (state[j][l] - begin[j][l])
                    odd_t = 0.5 * (state[j][HALF + l] - begin[j][HALF + l])
                    low_t, high_t = even_t + odd_t, even_t - odd_t
                    heat = heat + (low_t * low_t + high_t * high_t)
                    ob[r, at(l), :] = adv[r, at(l), :] + low_t
                    ob[r, at(LEV - 1 - l), :] = adv[r, at(LEV - 1 - l), :] + high_t
                heat8[r] = heat8[r] + heat
            return carry

        lax.fori_loop(0, RD // 2, pair, 0)

    for k in range(NC):
        for c in rows1[k] + cols1[k]:
            c.wait_recv()
        transport(1, k, q1, adv, merged(col_rx1[k, 0], col_rx1[k, 1]), False)
        if k == 0:
            rung(1, 4)
        if CHUNKS[k][1] == 8:
            physics(0)
    physics(1)

    heats = []
    for r in range(RD):
        heat = jnp.sum(heat8[r], axis=0, keepdims=True) * (1.0 / (NF * LEV))
        heats.append(jnp.broadcast_to(heat, (8, CD)))
    for t in range(n_wide // 8):
        hi, lo = zero, zero
        for r in range(RD):
            hi = hi + jnp.where(t_rows[r] == hib[t], heats[r], 0.0)
            lo = lo + jnp.where(t_rows[r] == lob[t], heats[r], 0.0)
        hi = jnp.broadcast_to(jnp.sum(hi, axis=1, keepdims=True), (8, CD))
        lo = jnp.broadcast_to(jnp.sum(lo, axis=1, keepdims=True), (8, CD))
        slots = jnp.where(lane == 2, hib[t], lob[t]) - ((t * 8 + sub) * CELLS).astype(F32)
        msg[t * 8 : t * 8 + 8, :] = jnp.where(lane == 0, hi, jnp.where(lane == 1, lo, slots))
    got[pl.ds(w, 1), :] = jnp.full((1, CD), -1.0, F32)

    rung(2, 0)

    def post(i, carry):
        m, dy = i // NY, i % NY
        dz = nz // 2 + (1 - 2 * (m % 2)) * ((m + 1) // 2)
        to = wide_at(dz, dy)
        pltpu.make_async_remote_copy(
            msg.at[pl.ds(to, 1)],
            got.at[pl.ds(w, 1)],
            msg_send,
            msg_recv,
            device_id={"wide": to},
            device_id_type=pl.DeviceIdType.MESH,
        ).start()
        return carry

    lax.fori_loop(0, n_wide - NY, post, 0)
    lax.fori_loop(n_wide - NY + 1, n_wide, post, 0)

    base = w * RD
    mine = zero
    wide_lane = lax.broadcasted_iota(jnp.int32, (CD, CD), 0)
    for r in range(RD):
        t_row = tgtb[r : r + 1, :]
        here = jnp.broadcast_to(t_row // CD - base, (8, CD))
        a = jnp.where((here == sub) & (sub < RD), heats[r], 0.0)
        b = jnp.where(jnp.broadcast_to(t_row % CD, (CD, CD)) == wide_lane, 1.0, 0.0)
        mine = mine + lax.dot_general(
            a, b, (((1,), (1,)), ((), ())), precision=HIGH, preferred_element_type=F32
        )

    mine_out[...] = mine
    for c in sends:
        c.wait_send()
    everyone = pl.ds(0, n_wide - 1)
    pltpu.make_async_copy(msg.at[everyone], got.at[everyone], msg_send).wait()
    pltpu.make_async_copy(msg.at[everyone], got.at[everyone], msg_recv).wait()
    got_out[...] = got[...]


def finish(n_wide, state, got, mine, out_hbm, span_hbm, spanb, out_sem, span_sem):
    copies = []
    for r in range(RD):
        c = pltpu.make_async_copy(
            state.at[r, pl.ds(0, NF * LEV)], out_hbm.at[:, r], out_sem.at[r]
        )
        c.start()
        copies.append(c)
    lane = lax.broadcasted_iota(jnp.int32, (8, CD), 1)
    sub = lax.broadcasted_iota(jnp.int32, (8, CD), 0)
    rows = [jnp.zeros((8, CD), F32) for r in range(RD)]
    place = [(lane + r * CD).astype(F32) for r in range(RD)]
    for t in range(n_wide // 8):
        tile = got[t * 8 : t * 8 + 8, :]
        value = [jnp.broadcast_to(tile[:, i : i + 1], (8, CD)) for i in range(2)]
        slot = [jnp.broadcast_to(tile[:, i + 2 : i + 3], (8, CD)) for i in range(2)]
        for r in range(RD):
            for i in range(2):
                rows[r] = rows[r] + jnp.where(slot[i] == place[r], value[i], 0.0)
    total = mine[...]
    for r in range(RD):
        arrived = jnp.broadcast_to(jnp.sum(rows[r], axis=0, keepdims=True), (8, CD))
        total = total + jnp.where(sub == r, arrived, 0.0)
    spanb[...] = total[0:RD]
    c = pltpu.make_async_copy(spanb, span_hbm, span_sem)
    c.start()
    for d in copies:
        d.wait()
    c.wait()


def body(n_wide, n_narrow, tracers, courant_x, courant_y, physics_ref, class_coeffs, span_target, cloud_class):
    anyspace = pl.BlockSpec(memory_space=pl.ANY)
    inside = pl.BlockSpec(memory_space=pltpu.VMEM)
    dma, regular = pltpu.SemaphoreType.DMA, pltpu.SemaphoreType.REGULAR
    vm = lambda *shape: pltpu.VMEM(shape, F32)
    tiles = n_wide // 8
    state, got, mine = pl.pallas_call(
        functools.partial(kernel, n_wide, n_narrow),
        out_shape=(
            vm(RD, FP * LEV, CD),
            vm(n_wide, CD),
            vm(8, CD),
        ),
        in_specs=[pl.BlockSpec(memory_space=pltpu.HBM)] * 7,
        out_specs=[inside] * 3,
        scratch_shapes=[
            vm(RD, NF * LEV, CD),
            vm(RD, NF * LEV, CD),
            vm(RD, FP * LEV, CD),
            vm(RD, LEV, CD),
            vm(RD, LEV, CD),
            vm(LEV, CD),
            vm(FP, LEV),
            vm(3, 2, NF),
            pltpu.VMEM((RD, CD), jnp.int32),
            pltpu.VMEM((RD, CD), jnp.int32),
            vm(2, NF * LEV, CD),
            vm(2, NF * LEV, CD),
            vm(2, 8, CD),
            vm(2, 2, 8, CD),
            vm(NC, 8, CD),
            vm(NC, 2, 8, CD),
            vm(5, RD, LEV, CD),
            vm(RD, 2, HALF + 1, 8, CD),
            vm(RD, 2, LEV, 8, CD),
            vm(RD, 2, HALF + 1, 8, CD),
            vm(tiles, 8, CD),
            vm(tiles, 8, CD),
            vm(RD, 8, CD),
            vm(n_wide, CD),
            vm(n_wide, CD),
            dma((NC, RD)),
            dma((12,)),
            dma((2, NC, 2)),
            dma((2, NC, 2)),
            dma,
            dma,
            dma((1 + NC, 2)),
            dma((1 + NC, 2)),
            dma,
            dma,
            regular((3,)),
        ],
        compiler_params=pltpu.CompilerParams(
            collective_id=0, has_side_effects=True
        ),
        name="transport_physics",
    )(
        tracers.reshape(NF * LEV, RD, CD),
        courant_x,
        courant_y,
        physics_ref,
        jnp.transpose(class_coeffs, (1, 0, 2)),
        span_target,
        cloud_class,
    )
    out, span = pl.pallas_call(
        functools.partial(finish, n_wide),
        out_shape=(
            jax.ShapeDtypeStruct((NF * LEV, RD, CD), F32),
            jax.ShapeDtypeStruct((RD, CD), F32),
        ),
        in_specs=[inside] * 3,
        out_specs=(anyspace, anyspace),
        scratch_shapes=[vm(RD, CD), dma((RD,)), dma],
        compiler_params=pltpu.CompilerParams(vmem_limit_bytes=4 << 20),
        name="finish",
    )(state, got, mine)
    return out.reshape(NF, LEV, RD, CD), span


def solution(mesh):
    return jax.shard_map(
        functools.partial(body, mesh.shape["wide"], mesh.shape["narrow"]),
        mesh=mesh,
        in_specs=(
            P(None, None, "wide", "narrow"),
            P(None, "wide", "narrow"),
            P(None, "wide", "narrow"),
            P(),
            P(),
            P("wide", "narrow"),
            P("wide", "narrow"),
        ),
        out_specs=(P(None, None, "wide", "narrow"), P("wide", "narrow")),
        check_vma=False,
    )
```

```python
import functools

import jax
import jax.numpy as jnp
from jax import lax
from jax.experimental import pallas as pl
from jax.experimental.pallas import tpu as pltpu
from jax.sharding import PartitionSpec as P

F32 = jnp.float32
NF, LEV, RD, CD = 13, 16, 4, 128
FP = 16
CELLS = RD * CD
HALF = LEV // 2
CHUNKS = ((0, 4), (4, 8), (8, 11), (11, 13))
NC = len(CHUNKS)
CX_AT, CY_AT = (0, 2, 3, 7), (1, 4, 5, 6)
NY = 4
HIGH = lax.Precision.HIGHEST


def kernel(
    n_wide,
    n_narrow,
    x_hbm,
    cx_hbm,
    cy_hbm,
    ref_hbm,
    cc_hbm,
    tgt_hbm,
    cls_hbm,
    ob,
    got_out,
    mine_out,
    q0,
    q1,
    adv,
    cb,
    cb_s,
    cb_n,
    refb,
    ccb,
    tgtb,
    clsb,
    halo_n,
    halo_s,
    edge_tx,
    edge_rx,
    corner_rx,
    coef,
    t_inv,
    t_b,
    t_c,
    hib,
    lob,
    heat8,
    msg,
    got,
    in_sem,
    small_sem,
    row_send,
    row_recv,
    cb_send,
    cb_recv,
    edge_send,
    edge_recv,
    corner_send,
    corner_recv,
    msg_send,
    msg_recv,
    ladder_sem,
    side_sem,
):
    nz = n_wide // NY
    w = lax.axis_index("wide")
    n = lax.axis_index("narrow")
    z, y = w // NY, w % NY

    def wide_at(dz, dy):
        return ((z + dz + nz) % nz) * NY + (y + dy) % NY

    north, south = (w + 1) % n_wide, (w + n_wide - 1) % n_wide
    east, west = (n + 1) % n_narrow, (n + n_narrow - 1) % n_narrow
    ladder = nz == 16

    barrier = pltpu.get_barrier_semaphore()

    def hello(**at):
        pl.semaphore_signal(barrier, 1, device_id=at, device_id_type=pl.DeviceIdType.MESH)

    hello(wide=north)
    hello(wide=south)
    hello(narrow=east)
    hello(narrow=west)
    hellos = 4
    if ladder:
        for dy in (1, 2, 3):
            hello(wide=wide_at(0, dy))
        for dz in (1, -1, 2, -2):
            hello(wide=wide_at(dz, 0))
        hellos += 7
    else:
        for i in range(1, n_wide):
            hello(wide=(w + i) % n_wide)
        hellos += n_wide - 1

    def fields(f0, f1):
        return pl.ds(f0 * LEV, (f1 - f0) * LEV)

    small = []

    def load(src, dst):
        c = pltpu.make_async_copy(src, dst, small_sem.at[len(small)])
        c.start()
        small.append(c)

    for r in range(RD):
        load(cx_hbm.at[:, r], cb.at[CX_AT[r]])
    for r in range(RD):
        load(cy_hbm.at[:, r], cb.at[CY_AT[r]])
    loads = []
    for k, (f0, f1) in enumerate(CHUNKS):
        for r in range(RD):
            c = pltpu.make_async_copy(
                x_hbm.at[fields(f0, f1), r],
                q0.at[r, fields(f0, f1)],
                in_sem.at[k, r],
            )
            c.start()
            loads.append(c)
    load(tgt_hbm, tgtb)
    load(cls_hbm, clsb)
    load(ref_hbm, refb.at[pl.ds(0, NF)])
    load(cc_hbm, ccb)

    lane = lax.broadcasted_iota(jnp.int32, (8, CD), 1)
    sub = lax.broadcasted_iota(jnp.int32, (8, CD), 0)
    first, last = lane == 0, lane == CD - 1
    edge = first | last
    inner = (lane == 1) | (lane == CD - 2)
    lane_row = ((lane + 1) // 2) % RD
    even = lane % 2 == 0
    zero = jnp.zeros((8, CD), F32)
    refb[NF:FP, :] = jnp.zeros((FP - NF, LEV), F32)
    adv[:, NF * LEV : FP * LEV, :] = jnp.zeros((RD, (FP - NF) * LEV, CD), F32)

    def spin(v, shift):
        shift %= CD
        return pltpu.roll(v, shift, 1) if shift else v

    def shift_of(r, f, h):
        return 2 * ((f % 8) * 8 + h * RD + r)

    def packed(v, r, f, h, which=None):
        return spin(jnp.where(edge if which is None else which, v, 0.0), shift_of(r, f, h))

    def halves(h, f=0):
        return pl.ds(f * LEV + h * 8, 8)

    for c in small[: 2 * RD]:
        c.wait()
    for c in loads:
        c.wait()

    def cx_at(r, h):
        return cb[CX_AT[r], halves(h), :]

    def cy_at(r, h):
        return cb[CY_AT[r], halves(h), :]

    for i in range(2):
        outer, second = [], []
        for r in range(RD):
            a, b = zero, zero
            for f in range(8 * i, min(8 * i + 8, NF)):
                for h in range(2):
                    v = q0[r, halves(h, f), :]
                    a = a + packed(v, r, f, h)
                    b = b + packed(v, r, f, h, inner)
            if i:
                for h in range(2):
                    a = a + packed(cx_at(r, h), r, NF, h)
                    b = b + packed(cx_at(r, h), r, NF, h, inner)
                    a = a + packed(cy_at(r, h), r, NF + 1, h)
            outer.append(a)
            second.append(b)
        edge_tx[i] = (outer[0] + outer[1]) + (outer[2] + outer[3])
        edge_tx[2 + i] = (second[0] + second[1]) + (second[2] + second[3])
    for c in small[2 * RD :]:
        c.wait()

    pl.semaphore_wait(barrier, hellos)

    sends = []

    def send(src, dst, ssem, rsem, **at):
        c = pltpu.make_async_remote_copy(
            src, dst, ssem, rsem, device_id=at, device_id_type=pl.DeviceIdType.MESH
        )
        c.start()
        sends.append(c)
        return c

    if ladder:
        for dz in (1, -1):
            pl.semaphore_signal(
                ladder_sem.at[0],
                1,
                device_id={"wide": wide_at(dz, 0)},
                device_id_type=pl.DeviceIdType.MESH,
            )

    def rung(i, dz):
        if ladder:
            pl.semaphore_wait(ladder_sem.at[i], 2)
            if dz:
                for s in (dz, -dz):
                    pl.semaphore_signal(
                        ladder_sem.at[i + 1],
                        1,
                        device_id={"wide": wide_at(s, 0)},
                        device_id_type=pl.DeviceIdType.MESH,
                    )

    def tell(sem, **at):
        pl.semaphore_signal(sem, 1, device_id=at, device_id_type=pl.DeviceIdType.MESH)

    tell(side_sem, narrow=east)
    tell(side_sem, narrow=west)

    def send_rows(k):
        part = fields(*CHUNKS[k])
        up = send(
            q0.at[pl.ds(RD - 2, 2), part],
            halo_s.at[:, part],
            row_send.at[k, 0],
            row_recv.at[k, 0],
            wide=north,
        )
        down = send(
            q0.at[pl.ds(0, 2), part],
            halo_n.at[:, part],
            row_send.at[k, 1],
            row_recv.at[k, 1],
            wide=south,
        )
        return (up, down)

    faces = (
        send(cb.at[pl.ds(5, 3)], cb_s, cb_send.at[0], cb_recv.at[0], wide=north),
        send(cb.at[pl.ds(0, 2)], cb_n, cb_send.at[1], cb_recv.at[1], wide=south),
    )
    rows = [send_rows(0)]
    edges = (
        send(edge_tx, edge_rx.at[0], edge_send.at[0], edge_recv.at[0], narrow=east),
        send(edge_tx, edge_rx.at[1], edge_send.at[1], edge_recv.at[1], narrow=west),
    )
    rows.append(send_rows(1))
    pl.semaphore_wait(side_sem, 2)
    corners = []
    for i, (ns, ew) in enumerate(((north, east), (north, west), (south, east), (south, west))):
        corners.append(
            send(
                edge_tx.at[pl.ds(0, 2)],
                corner_rx.at[i],
                corner_send.at[i],
                corner_recv.at[i],
                wide=ns,
                narrow=ew,
            )
        )
    rows += [send_rows(k) for k in range(2, NC)]
    rung(0, 3)

    fsub = lax.broadcasted_iota(jnp.int32, (FP, NF), 0)
    flane = lax.broadcasted_iota(jnp.int32, (FP, NF), 1)
    by_class = []
    for k in range(3):
        pair = []
        for j in range(2):
            row = jnp.broadcast_to(ccb[k, j : j + 1, :], (FP, NF))
            column = jnp.sum(jnp.where(fsub == flane, row, 0.0), axis=1, keepdims=True)
            column = column / float((1, 2, 4)[k])
            pair.append([jnp.broadcast_to(column[g * 8 : g * 8 + 8], (8, CD)) for g in range(2)])
        by_class.append(pair)

    def class_row(r):
        return jnp.broadcast_to(clsb[pl.ds(r, 1), :], (8, CD))

    for g in range(2):
        refs = refb[g * 8 : g * 8 + 8, :]

        def tables(r, carry, g=g, refs=refs):
            kind = class_row(r)
            pick = lambda j: jnp.where(
                kind == 2,
                by_class[2][j][g],
                jnp.where(kind == 1, by_class[1][j][g], by_class[0][j][g]),
            )
            d, rate = pick(0), pick(1)
            middle = 1.0 + rate + 2.0 * d
            ratio = None
            for l in range(HALF):
                diagonal = middle if l else 1.0 + rate + d
                denominator = diagonal - d * ratio if l else diagonal
                level = [jnp.broadcast_to(refs[:, m : m + 1], (8, CD)) for m in (l, LEV - 1 - l)]
                even_ref, odd_ref = rate * (level[0] + level[1]), rate * (level[0] - level[1])
                if l < HALF - 1:
                    inverse = 1.0 / denominator
                    ratio = d * inverse
                    t_inv[r, g, l] = inverse
                    t_c[r, g, l] = ratio
                    t_b[r, g, l] = even_ref * inverse
                    t_b[r, g, HALF + l] = odd_ref * inverse
                else:
                    even_inv, odd_inv = 1.0 / (denominator - d), 1.0 / (denominator + d)
                    t_inv[r, g, l] = even_inv
                    t_inv[r, g, l + 1] = odd_inv
                    t_c[r, g, l] = d * even_inv
                    t_c[r, g, l + 1] = d * odd_inv
                    t_b[r, g, l] = even_ref * even_inv
                    t_b[r, g, HALF + l] = odd_ref * odd_inv
            return carry

        lax.fori_loop(0, RD, tables, 0)

    target_f = tgtb[...].astype(F32)
    t_rows = [jnp.broadcast_to(target_f[r : r + 1], (8, CD)) for r in range(RD)]
    o_rows = [jnp.broadcast_to(tgtb[r : r + 1, :] // CELLS, (8, CD)) for r in range(RD)]

    def ends(t, carry):
        d = t * 8 + sub
        hi = jnp.full((8, CD), -1.0, F32)
        lo = jnp.full((8, CD), 1e9, F32)
        for r in range(RD):
            hit = o_rows[r] == d
            hi = jnp.maximum(hi, jnp.where(hit, t_rows[r], -1.0))
            lo = jnp.minimum(lo, jnp.where(hit, t_rows[r], 1e9))
        hib[t] = jnp.broadcast_to(jnp.max(hi, axis=1, keepdims=True), (8, CD))
        lob[t] = jnp.broadcast_to(jnp.min(lo, axis=1, keepdims=True), (8, CD))
        return carry

    lax.fori_loop(0, n_wide // 8, ends, 0)

    def merged(from_west, from_east, by_west, by_east):
        return jnp.where(even, spin(from_west, by_west), spin(from_east, by_east))

    def weights(east_x, west_x, north_y, south_y):
        return (
            1.0
            - jnp.maximum(east_x, 0.0)
            + jnp.minimum(west_x, 0.0)
            - jnp.maximum(north_y, 0.0)
            + jnp.minimum(south_y, 0.0),
            -jnp.minimum(east_x, 0.0),
            jnp.maximum(west_x, 0.0),
            -jnp.minimum(north_y, 0.0),
            jnp.maximum(south_y, 0.0),
        )

    def keep_weights(r, h, values):
        for i, v in enumerate(values):
            coef[i, r + 1, halves(h), :] = v

    def stencil(c, here, north_q, south_q, around):
        east_q = jnp.where(last, around, spin(here, -1))
        west_q = jnp.where(first, around, spin(here, 1))
        return ((c[0] * here + c[3] * north_q) + c[4] * south_q) + (c[1] * east_q + c[2] * west_q)

    edges[0].wait_recv()
    edges[1].wait_recv()
    near = [merged(edge_rx[0, i], edge_rx[1, i], 1, -1) for i in range(2)]
    deep = [merged(edge_rx[0, 2 + i], edge_rx[1, 2 + i], 2, -2) for i in range(2)]
    faces[0].wait_recv()
    faces[1].wait_recv()
    for h in range(2):
        for r in range(RD):
            east_x = cx_at(r, h)
            around = spin(near[1], -shift_of(r, NF, h))
            west_x = jnp.where(first, around, spin(east_x, 1))
            south_y = cy_at(r - 1, h) if r else cb_s[1, halves(h), :]
            keep_weights(r, h, weights(east_x, west_x, cy_at(r, h), south_y))

    for k, (f0, f1) in enumerate(CHUNKS):
        for c in rows[k]:
            c.wait_recv()
        for h in range(2):
            for r in range(RD):
                c = [coef[i, r + 1, halves(h), :] for i in range(5)]
                for f in range(f0, f1):
                    at = halves(h, f)
                    q1[r + 1, at, :] = stencil(
                        c,
                        q0[r, at, :],
                        q0[r + 1, at, :] if r < RD - 1 else halo_n[0, at, :],
                        q0[r - 1, at, :] if r else halo_s[1, at, :],
                        spin(near[f // 8], -shift_of(r, f, h)),
                    )
        if k == 1:
            rung(1, 4)

    for c in corners:
        c.wait_recv()
    below = [merged(corner_rx[0, i], corner_rx[1, i], -5, -7) for i in range(2)]
    above = [merged(corner_rx[2, i], corner_rx[3, i], 7, 5) for i in range(2)]
    cx_shift, cy_shift = -16 * (NF % 8), -16 * (NF % 8 + 1)
    side_y = spin(near[1], cy_shift)
    side = []
    for v in weights(
        spin(near[1], cx_shift),
        jnp.where(even, spin(deep[1], cx_shift), spin(edge_tx[1], cx_shift)),
        side_y,
        jnp.where(lane_row == 0, spin(below[1], cy_shift), spin(side_y, 2)),
    ):
        v = jnp.where((lane + 1) % CD < 16, v, 0.0)
        for by in (16, 32, 64):
            v = v + spin(v, by)
        side.append(v)
    beside = []
    for i in range(2):
        own = edge_tx[i]
        beside.append(
            side[0] * near[i]
            + side[1] * jnp.where(even, own, deep[i])
            + side[2] * jnp.where(even, deep[i], own)
            + side[3] * jnp.where(lane_row == RD - 1, above[i], spin(near[i], -2))
            + side[4] * jnp.where(lane_row == 0, below[i], spin(near[i], 2))
        )
    for h in range(2):
        for r, east_x, corner, north_y, south_y in (
            (-1, cb_s[2, halves(h), :], below, cb_s[1, halves(h), :], cb_s[0, halves(h), :]),
            (RD, cb_n[0, halves(h), :], above, cb_n[1, halves(h), :], cy_at(RD - 1, h)),
        ):
            around = spin(corner[1], -shift_of(max(0, min(r, RD - 1)), NF, h))
            west_x = jnp.where(first, around, spin(east_x, 1))
            keep_weights(r, h, weights(east_x, west_x, north_y, south_y))

    def complete(k):
        f0, f1 = CHUNKS[k]
        for h in range(2):
            low = [coef[i, 0, halves(h), :] for i in range(5)]
            high = [coef[i, RD + 1, halves(h), :] for i in range(5)]
            for f in range(f0, f1):
                at = halves(h, f)
                q1[0, at, :] = stencil(
                    low,
                    halo_s[1, at, :],
                    q0[0, at, :],
                    halo_s[0, at, :],
                    spin(below[f // 8], -shift_of(0, f, h)),
                )
                q1[RD + 1, at, :] = stencil(
                    high,
                    halo_n[0, at, :],
                    halo_n[1, at, :],
                    q0[RD - 1, at, :],
                    spin(above[f // 8], -shift_of(RD - 1, f, h)),
                )
        for h in range(2):
            for r in range(RD):
                c = [coef[i, r + 1, halves(h), :] for i in range(5)]
                for f in range(f0, f1):
                    at = halves(h, f)
                    adv[r, at, :] = stencil(
                        c,
                        q1[r + 1, at, :],
                        q1[r + 2, at, :],
                        q1[r, at, :],
                        spin(beside[f // 8], -shift_of(r, f, h)),
                    )

    for r in range(RD):
        heat8[r] = zero

    def physics(g):
        def at(l):
            return pl.ds(g * 8 * LEV + l, 8, stride=LEV)

        def pair(i, carry):
            rows = [2 * i, 2 * i + 1]
            kinds = [class_row(r) for r in rows]
            begin = []
            for r in rows:
                low = [adv[r, at(l), :] for l in range(HALF)]
                high = [adv[r, at(LEV - 1 - l), :] for l in range(HALF)]
                begin.append([a + b for a, b in zip(low, high)] + [a - b for a, b in zip(low, high)])
            state = [list(b) for b in begin]
            for s in range(4):
                part = [[None] * LEV for r in rows]
                for l in range(HALF):
                    for j, r in enumerate(rows):
                        for odd in range(2):
                            m = odd * HALF + l
                            v = state[j][m] * t_inv[r, g, l + (odd if l == HALF - 1 else 0)]
                            v = v + t_b[r, g, m]
                            if l:
                                own = l + (odd if l == HALF - 1 else 0)
                                v = v + t_c[r, g, own] * part[j][m - 1]
                            part[j][m] = v
                for l in range(HALF - 2, -1, -1):
                    for j, r in enumerate(rows):
                        for odd in range(2):
                            m = odd * HALF + l
                            part[j][m] = part[j][m] + t_c[r, g, l] * part[j][m + 1]
                for j in range(2):
                    if s:
                        keep = kinds[j] >= (1 if s == 1 else 2)
                        part[j] = [jnp.where(keep, a, b) for a, b in zip(part[j], state[j])]
                    state[j] = part[j]
            for j, r in enumerate(rows):
                heat = zero
                for l in range(HALF):
                    even_t = 0.5 * (state[j][l] - begin[j][l])
                    odd_t = 0.5 * (state[j][HALF + l] - begin[j][HALF + l])
                    low_t, high_t = even_t + odd_t, even_t - odd_t
                    heat = heat + (low_t * low_t + high_t * high_t)
                    ob[r, at(l), :] = adv[r, at(l), :] + low_t
                    ob[r, at(LEV - 1 - l), :] = adv[r, at(LEV - 1 - l), :] + high_t
                heat8[r] = heat8[r] + heat
            return carry

        lax.fori_loop(0, RD // 2, pair, 0)

    for k in range(NC):
        complete(k)
        if CHUNKS[k][1] == 8:
            physics(0)
    physics(1)

    heats = []
    for r in range(RD):
        heat = jnp.sum(heat8[r], axis=0, keepdims=True) * (1.0 / (NF * LEV))
        heats.append(jnp.broadcast_to(heat, (8, CD)))
    for t in range(n_wide // 8):
        hi, lo = zero, zero
        for r in range(RD):
            hi = hi + jnp.where(t_rows[r] == hib[t], heats[r], 0.0)
            lo = lo + jnp.where(t_rows[r] == lob[t], heats[r], 0.0)
        hi = jnp.broadcast_to(jnp.sum(hi, axis=1, keepdims=True), (8, CD))
        lo = jnp.broadcast_to(jnp.sum(lo, axis=1, keepdims=True), (8, CD))
        slots = jnp.where(lane == 2, hib[t], lob[t]) - ((t * 8 + sub) * CELLS).astype(F32)
        msg[t * 8 : t * 8 + 8, :] = jnp.where(lane == 0, hi, jnp.where(lane == 1, lo, slots))
    got[pl.ds(w, 1), :] = jnp.full((1, CD), -1.0, F32)

    rung(2, 0)

    def post(i, carry):
        m, dy = i // NY, i % NY
        dz = nz // 2 + (1 - 2 * (m % 2)) * ((m + 1) // 2)
        to = wide_at(dz, dy)
        pltpu.make_async_remote_copy(
            msg.at[pl.ds(to, 1)],
            got.at[pl.ds(w, 1)],
            msg_send,
            msg_recv,
            device_id={"wide": to},
            device_id_type=pl.DeviceIdType.MESH,
        ).start()
        return carry

    lax.fori_loop(0, n_wide - NY, post, 0)
    lax.fori_loop(n_wide - NY + 1, n_wide, post, 0)

    base = w * RD
    mine = zero
    wide_lane = lax.broadcasted_iota(jnp.int32, (CD, CD), 0)
    for r in range(RD):
        t_row = tgtb[r : r + 1, :]
        here = jnp.broadcast_to(t_row // CD - base, (8, CD))
        a = jnp.where((here == sub) & (sub < RD), heats[r], 0.0)
        b = jnp.where(jnp.broadcast_to(t_row % CD, (CD, CD)) == wide_lane, 1.0, 0.0)
        mine = mine + lax.dot_general(
            a, b, (((1,), (1,)), ((), ())), precision=HIGH, preferred_element_type=F32
        )

    mine_out[...] = mine
    for c in sends:
        c.wait_send()
    everyone = pl.ds(0, n_wide - 1)
    pltpu.make_async_copy(msg.at[everyone], got.at[everyone], msg_send).wait()
    pltpu.make_async_copy(msg.at[everyone], got.at[everyone], msg_recv).wait()
    got_out[...] = got[...]


def finish(n_wide, state, got, mine, out_hbm, span_hbm, spanb, out_sem, span_sem):
    copies = []
    for r in range(RD):
        c = pltpu.make_async_copy(
            state.at[r, pl.ds(0, NF * LEV)], out_hbm.at[:, r], out_sem.at[r]
        )
        c.start()
        copies.append(c)
    lane = lax.broadcasted_iota(jnp.int32, (8, CD), 1)
    sub = lax.broadcasted_iota(jnp.int32, (8, CD), 0)
    rows = [jnp.zeros((8, CD), F32) for r in range(RD)]
    place = [(lane + r * CD).astype(F32) for r in range(RD)]
    for t in range(n_wide // 8):
        tile = got[t * 8 : t * 8 + 8, :]
        value = [jnp.broadcast_to(tile[:, i : i + 1], (8, CD)) for i in range(2)]
        slot = [jnp.broadcast_to(tile[:, i + 2 : i + 3], (8, CD)) for i in range(2)]
        for r in range(RD):
            for i in range(2):
                rows[r] = rows[r] + jnp.where(slot[i] == place[r], value[i], 0.0)
    total = mine[...]
    for r in range(RD):
        arrived = jnp.broadcast_to(jnp.sum(rows[r], axis=0, keepdims=True), (8, CD))
        total = total + jnp.where(sub == r, arrived, 0.0)
    spanb[...] = total[0:RD]
    c = pltpu.make_async_copy(spanb, span_hbm, span_sem)
    c.start()
    for d in copies:
        d.wait()
    c.wait()


def body(n_wide, n_narrow, tracers, courant_x, courant_y, physics_ref, class_coeffs, span_target, cloud_class):
    anyspace = pl.BlockSpec(memory_space=pl.ANY)
    inside = pl.BlockSpec(memory_space=pltpu.VMEM)
    dma, regular = pltpu.SemaphoreType.DMA, pltpu.SemaphoreType.REGULAR
    vm = lambda *shape: pltpu.VMEM(shape, F32)
    tiles = n_wide // 8
    state, got, mine = pl.pallas_call(
        functools.partial(kernel, n_wide, n_narrow),
        out_shape=(
            vm(RD, FP * LEV, CD),
            vm(n_wide, CD),
            vm(8, CD),
        ),
        in_specs=[pl.BlockSpec(memory_space=pltpu.HBM)] * 7,
        out_specs=[inside] * 3,
        scratch_shapes=[
            vm(RD, NF * LEV, CD),
            vm(RD + 2, NF * LEV, CD),
            vm(RD, FP * LEV, CD),
            vm(2 * RD, LEV, CD),
            vm(3, LEV, CD),
            vm(2, LEV, CD),
            vm(FP, LEV),
            vm(3, 2, NF),
            pltpu.VMEM((RD, CD), jnp.int32),
            pltpu.VMEM((RD, CD), jnp.int32),
            vm(2, NF * LEV, CD),
            vm(2, NF * LEV, CD),
            vm(4, 8, CD),
            vm(2, 4, 8, CD),
            vm(4, 2, 8, CD),
            vm(5, RD + 2, LEV, CD),
            vm(RD, 2, HALF + 1, 8, CD),
            vm(RD, 2, LEV, 8, CD),
            vm(RD, 2, HALF + 1, 8, CD),
            vm(tiles, 8, CD),
            vm(tiles, 8, CD),
            vm(RD, 8, CD),
            vm(n_wide, CD),
            vm(n_wide, CD),
            dma((NC, RD)),
            dma((12,)),
            dma((NC, 2)),
            dma((NC, 2)),
            dma((2,)),
            dma((2,)),
            dma((2,)),
            dma((2,)),
            dma((4,)),
            dma((4,)),
            dma,
            dma,
            regular((3,)),
            regular,
        ],
        compiler_params=pltpu.CompilerParams(
            collective_id=0, has_side_effects=True
        ),
        name="transport_physics",
    )(
        tracers.reshape(NF * LEV, RD, CD),
        courant_x,
        courant_y,
        physics_ref,
        jnp.transpose(class_coeffs, (1, 0, 2)),
        span_target,
        cloud_class,
    )
    out, span = pl.pallas_call(
        functools.partial(finish, n_wide),
        out_shape=(
            jax.ShapeDtypeStruct((NF * LEV, RD, CD), F32),
            jax.ShapeDtypeStruct((RD, CD), F32),
        ),
        in_specs=[inside] * 3,
        out_specs=(anyspace, anyspace),
        scratch_shapes=[vm(RD, CD), dma((RD,)), dma],
        compiler_params=pltpu.CompilerParams(vmem_limit_bytes=4 << 20),
        name="finish",
    )(state, got, mine)
    return out.reshape(NF, LEV, RD, CD), span


def solution(mesh):
    return jax.shard_map(
        functools.partial(body, mesh.shape["wide"], mesh.shape["narrow"]),
        mesh=mesh,
        in_specs=(
            P(None, None, "wide", "narrow"),
            P(None, "wide", "narrow"),
            P(None, "wide", "narrow"),
            P(),
            P(),
            P("wide", "narrow"),
            P("wide", "narrow"),
        ),
        out_specs=(P(None, None, "wide", "narrow"), P("wide", "narrow")),
        check_vma=False,
    )
```

```python
import functools

import jax
import jax.numpy as jnp
from jax import lax
from jax.experimental import pallas as pl
from jax.experimental.pallas import tpu as pltpu
from jax.sharding import PartitionSpec as P

F32 = jnp.float32
NF, LEV, RD, CD = 13, 16, 4, 128
CELLS = RD * CD
HALF = LEV // 2
CHUNKS = ((0, 4), (4, 8), (8, 11), (11, 13))
NC = len(CHUNKS)
SETS = tuple((k, s) for k, (f0, f1) in enumerate(CHUNKS) for s in range(-(-RD * (f1 - f0) // 8)))
BASE = tuple(128 * [q[0] for q in SETS].index(k) for k in range(NC))
CX_AT, CY_AT = (0, 2, 3, 7), (1, 4, 5, 6)
NY = 4
HIGH = lax.Precision.HIGHEST


def kernel(
    n_wide,
    n_narrow,
    x_hbm,
    cx_hbm,
    cy_hbm,
    ref_hbm,
    cc_hbm,
    tgt_hbm,
    cls_hbm,
    ob,
    got_out,
    mine_out,
    q0,
    q1,
    adv,
    cb,
    cb_s,
    cb_n,
    refb,
    ccb,
    tgtb,
    clsb,
    halo_n,
    halo_s,
    edge_tx,
    edge_rx,
    corner_rx,
    coef,
    t_inv,
    t_b,
    t_c,
    hib,
    lob,
    msg,
    got,
    in_sem,
    small_sem,
    row_send,
    row_recv,
    cb_send,
    cb_recv,
    edge_send,
    edge_recv,
    corner_send,
    corner_recv,
    msg_send,
    msg_recv,
    ladder_sem,
    side_sem,
):
    nz = n_wide // NY
    w = lax.axis_index("wide")
    n = lax.axis_index("narrow")
    z, y = w // NY, w % NY

    def wide_at(dz, dy):
        return ((z + dz + nz) % nz) * NY + (y + dy) % NY

    north, south = (w + 1) % n_wide, (w + n_wide - 1) % n_wide
    east, west = (n + 1) % n_narrow, (n + n_narrow - 1) % n_narrow
    ladder = nz == 16

    barrier = pltpu.get_barrier_semaphore()

    def hello(**at):
        pl.semaphore_signal(barrier, 1, device_id=at, device_id_type=pl.DeviceIdType.MESH)

    hello(wide=north)
    hello(wide=south)
    hello(narrow=east)
    hello(narrow=west)
    hellos = 4
    if ladder:
        for dy in (1, 2, 3):
            hello(wide=wide_at(0, dy))
        for dz in (1, -1, 2, -2):
            hello(wide=wide_at(dz, 0))
        hellos += 7
    else:
        for i in range(1, n_wide):
            hello(wide=(w + i) % n_wide)
        hellos += n_wide - 1

    def fields(f0, f1):
        return pl.ds(f0 * LEV, (f1 - f0) * LEV)

    small = []

    def load(src, dst):
        c = pltpu.make_async_copy(src, dst, small_sem.at[len(small)])
        c.start()
        small.append(c)

    for r in range(RD):
        load(cx_hbm.at[:, r], cb.at[CX_AT[r]])
    for r in range(RD):
        load(cy_hbm.at[:, r], cb.at[CY_AT[r]])
    loads = []
    for k, (f0, f1) in enumerate(CHUNKS):
        for r in range(RD):
            c = pltpu.make_async_copy(
                x_hbm.at[fields(f0, f1), r],
                q0.at[r, fields(f0, f1)],
                in_sem.at[k, r],
            )
            c.start()
            loads.append(c)
    load(tgt_hbm, tgtb)
    load(cls_hbm, clsb)
    load(ref_hbm, refb)
    load(cc_hbm, ccb)

    lane = lax.broadcasted_iota(jnp.int32, (8, CD), 1)
    sub = lax.broadcasted_iota(jnp.int32, (8, CD), 0)
    first, last = lane == 0, lane == CD - 1
    edge = first | last
    inner = (lane == 1) | (lane == CD - 2)
    lane_row = ((lane + 1) // 2) % RD
    even = lane % 2 == 0
    zero = jnp.zeros((8, CD), F32)
    for k, (f0, f1) in enumerate(CHUNKS):
        start, stop = BASE[k] + RD * (f1 - f0) * LEV, (BASE + (128 * len(SETS),))[k + 1]
        if stop > start:
            adv[start:stop, :] = jnp.zeros((stop - start, CD), F32)

    def spin(v, shift):
        shift %= CD
        return pltpu.roll(v, shift, 1) if shift else v

    def shift_of(r, f, h):
        return 2 * ((f % 8) * 8 + h * RD + r)

    def packed(v, r, f, h, which=None):
        return spin(jnp.where(edge if which is None else which, v, 0.0), shift_of(r, f, h))

    def halves(h, f=0):
        return pl.ds(f * LEV + h * 8, 8)

    for c in small[: 2 * RD]:
        c.wait()
    for c in loads:
        c.wait()

    def cx_at(r, h):
        return cb[CX_AT[r], halves(h), :]

    def cy_at(r, h):
        return cb[CY_AT[r], halves(h), :]

    for i in range(2):
        outer, second = [], []
        for r in range(RD):
            a, b = zero, zero
            for f in range(8 * i, min(8 * i + 8, NF)):
                for h in range(2):
                    v = q0[r, halves(h, f), :]
                    a = a + packed(v, r, f, h)
                    b = b + packed(v, r, f, h, inner)
            if i:
                for h in range(2):
                    a = a + packed(cx_at(r, h), r, NF, h)
                    b = b + packed(cx_at(r, h), r, NF, h, inner)
                    a = a + packed(cy_at(r, h), r, NF + 1, h)
            outer.append(a)
            second.append(b)
        edge_tx[i] = (outer[0] + outer[1]) + (outer[2] + outer[3])
        edge_tx[2 + i] = (second[0] + second[1]) + (second[2] + second[3])
    for c in small[2 * RD :]:
        c.wait()

    pl.semaphore_wait(barrier, hellos)

    sends = []

    def send(src, dst, ssem, rsem, **at):
        c = pltpu.make_async_remote_copy(
            src, dst, ssem, rsem, device_id=at, device_id_type=pl.DeviceIdType.MESH
        )
        c.start()
        sends.append(c)
        return c

    if ladder:
        for dz in (1, -1):
            pl.semaphore_signal(
                ladder_sem.at[0],
                1,
                device_id={"wide": wide_at(dz, 0)},
                device_id_type=pl.DeviceIdType.MESH,
            )

    def rung(i, dz):
        if ladder:
            pl.semaphore_wait(ladder_sem.at[i], 2)
            if dz:
                for s in (dz, -dz):
                    pl.semaphore_signal(
                        ladder_sem.at[i + 1],
                        1,
                        device_id={"wide": wide_at(s, 0)},
                        device_id_type=pl.DeviceIdType.MESH,
                    )

    def tell(sem, **at):
        pl.semaphore_signal(sem, 1, device_id=at, device_id_type=pl.DeviceIdType.MESH)

    tell(side_sem, narrow=east)
    tell(side_sem, narrow=west)

    def send_rows(k):
        part = fields(*CHUNKS[k])
        up = send(
            q0.at[pl.ds(RD - 2, 2), part],
            halo_s.at[:, part],
            row_send.at[k, 0],
            row_recv.at[k, 0],
            wide=north,
        )
        down = send(
            q0.at[pl.ds(0, 2), part],
            halo_n.at[:, part],
            row_send.at[k, 1],
            row_recv.at[k, 1],
            wide=south,
        )
        return (up, down)

    faces = (
        send(cb.at[pl.ds(5, 3)], cb_s, cb_send.at[0], cb_recv.at[0], wide=north),
        send(cb.at[pl.ds(0, 2)], cb_n, cb_send.at[1], cb_recv.at[1], wide=south),
    )
    rows = [send_rows(0)]
    edges = (
        send(edge_tx, edge_rx.at[0], edge_send.at[0], edge_recv.at[0], narrow=east),
        send(edge_tx, edge_rx.at[1], edge_send.at[1], edge_recv.at[1], narrow=west),
    )
    pl.semaphore_wait(side_sem, 2)
    corners = []
    for i, (ns, ew) in enumerate(((north, east), (north, west), (south, east), (south, west))):
        corners.append(
            send(
                edge_tx.at[pl.ds(0, 2)],
                corner_rx.at[i],
                corner_send.at[i],
                corner_recv.at[i],
                wide=ns,
                narrow=ew,
            )
        )
    rows += [send_rows(k) for k in range(1, NC)]
    rung(0, 3)

    class_rows = [jnp.broadcast_to(clsb[r : r + 1, :], (8, CD)) for r in range(RD)]

    def pairs_of(k, s, shape):
        f0, f1 = CHUNKS[k]
        at = 8 * s + lax.broadcasted_iota(jnp.int32, shape, 0)
        return at // (f1 - f0), jnp.where(at < RD * (f1 - f0), f0 + at % (f1 - f0), -1)

    kinds, row_of = [], []
    for q, (k, s) in enumerate(SETS):
        f0, f1 = CHUNKS[k]
        row, _ = pairs_of(k, s, (8, CD))
        kind = class_rows[0]
        for r in range(1, RD):
            kind = jnp.where(row == r, class_rows[r], kind)
        kinds.append(kind)
        row_of.append(row)
        _, field = pairs_of(k, s, (8, NF))
        hit = field == lax.broadcasted_iota(jnp.int32, (8, NF), 1)

        def column(category, j, hit=hit):
            row = jnp.broadcast_to(ccb[category, j : j + 1, :], (8, NF))
            total = jnp.sum(jnp.where(hit, row, 0.0), axis=1, keepdims=True)
            return jnp.broadcast_to(total * (1.0, 0.5, 0.25)[category], (8, CD))

        d, rate = (
            jnp.where(kind == 2, column(2, j), jnp.where(kind == 1, column(1, j), column(0, j)))
            for j in range(2)
        )
        _, field = pairs_of(k, s, (8, LEV))
        refs = jnp.zeros((8, LEV), F32)
        for f in range(f0, f1):
            refs = jnp.where(field == f, jnp.broadcast_to(refb[f : f + 1, :], (8, LEV)), refs)
        middle = 1.0 + rate + 2.0 * d
        ratio = None
        for l in range(HALF):
            diagonal = middle if l else 1.0 + rate + d
            denominator = diagonal - d * ratio if l else diagonal
            level = [jnp.broadcast_to(refs[:, m : m + 1], (8, CD)) for m in (l, LEV - 1 - l)]
            even_ref, odd_ref = rate * (level[0] + level[1]), rate * (level[0] - level[1])
            if l < HALF - 1:
                inverse = 1.0 / denominator
                ratio = d * inverse
                t_inv[q, l] = inverse
                t_c[q, l] = ratio
                t_b[q, l] = even_ref * inverse
                t_b[q, HALF + l] = odd_ref * inverse
            else:
                even_inv, odd_inv = 1.0 / (denominator - d), 1.0 / (denominator + d)
                t_inv[q, l] = even_inv
                t_inv[q, l + 1] = odd_inv
                t_c[q, l] = d * even_inv
                t_c[q, l + 1] = d * odd_inv
                t_b[q, l] = even_ref * even_inv
                t_b[q, HALF + l] = odd_ref * odd_inv

    target_f = tgtb[...].astype(F32)
    t_rows = [jnp.broadcast_to(target_f[r : r + 1], (8, CD)) for r in range(RD)]
    o_rows = [jnp.broadcast_to(tgtb[r : r + 1, :] // CELLS, (8, CD)) for r in range(RD)]

    def ends(t, carry):
        d = t * 8 + sub
        hi = jnp.full((8, CD), -1.0, F32)
        lo = jnp.full((8, CD), 1e9, F32)
        for r in range(RD):
            hit = o_rows[r] == d
            hi = jnp.maximum(hi, jnp.where(hit, t_rows[r], -1.0))
            lo = jnp.minimum(lo, jnp.where(hit, t_rows[r], 1e9))
        hib[t] = jnp.broadcast_to(jnp.max(hi, axis=1, keepdims=True), (8, CD))
        lob[t] = jnp.broadcast_to(jnp.min(lo, axis=1, keepdims=True), (8, CD))
        return carry

    lax.fori_loop(0, n_wide // 8, ends, 0)

    def merged(from_west, from_east, by_west, by_east):
        return jnp.where(even, spin(from_west, by_west), spin(from_east, by_east))

    def weights(east_x, west_x, north_y, south_y):
        return (
            1.0
            - jnp.maximum(east_x, 0.0)
            + jnp.minimum(west_x, 0.0)
            - jnp.maximum(north_y, 0.0)
            + jnp.minimum(south_y, 0.0),
            -jnp.minimum(east_x, 0.0),
            jnp.maximum(west_x, 0.0),
            -jnp.minimum(north_y, 0.0),
            jnp.maximum(south_y, 0.0),
        )

    def keep_weights(r, h, values):
        for i, v in enumerate(values):
            coef[i, r + 1, halves(h), :] = v

    def stencil(c, here, north_q, south_q, around):
        east_q = jnp.where(last, around, spin(here, -1))
        west_q = jnp.where(first, around, spin(here, 1))
        return ((c[0] * here + c[3] * north_q) + c[4] * south_q) + (c[1] * east_q + c[2] * west_q)

    edges[0].wait_recv()
    edges[1].wait_recv()
    near = [merged(edge_rx[0, i], edge_rx[1, i], 1, -1) for i in range(2)]
    deep = [merged(edge_rx[0, 2 + i], edge_rx[1, 2 + i], 2, -2) for i in range(2)]
    faces[0].wait_recv()
    faces[1].wait_recv()
    for h in range(2):
        for r in range(RD):
            east_x = cx_at(r, h)
            around = spin(near[1], -shift_of(r, NF, h))
            west_x = jnp.where(first, around, spin(east_x, 1))
            south_y = cy_at(r - 1, h) if r else cb_s[1, halves(h), :]
            keep_weights(r, h, weights(east_x, west_x, cy_at(r, h), south_y))

    def own_step(k):
        f0, f1 = CHUNKS[k]
        for c in rows[k]:
            c.wait_recv()
        for h in range(2):
            for r in range(RD):
                c = [coef[i, r + 1, halves(h), :] for i in range(5)]
                for f in range(f0, f1):
                    at = halves(h, f)
                    q1[r + 1, at, :] = stencil(
                        c,
                        q0[r, at, :],
                        q0[r + 1, at, :] if r < RD - 1 else halo_n[0, at, :],
                        q0[r - 1, at, :] if r else halo_s[1, at, :],
                        spin(near[f // 8], -shift_of(r, f, h)),
                    )

    rung(1, 4)
    own_step(0)

    for c in corners:
        c.wait_recv()
    below = [merged(corner_rx[0, i], corner_rx[1, i], -5, -7) for i in range(2)]
    above = [merged(corner_rx[2, i], corner_rx[3, i], 7, 5) for i in range(2)]
    cx_shift, cy_shift = -16 * (NF % 8), -16 * (NF % 8 + 1)
    side_y = spin(near[1], cy_shift)
    side = []
    for v in weights(
        spin(near[1], cx_shift),
        jnp.where(even, spin(deep[1], cx_shift), spin(edge_tx[1], cx_shift)),
        side_y,
        jnp.where(lane_row == 0, spin(below[1], cy_shift), spin(side_y, 2)),
    ):
        v = jnp.where((lane + 1) % CD < 16, v, 0.0)
        for by in (16, 32, 64):
            v = v + spin(v, by)
        side.append(v)
    beside = []
    for i in range(2):
        own = edge_tx[i]
        beside.append(
            side[0] * near[i]
            + side[1] * jnp.where(even, own, deep[i])
            + side[2] * jnp.where(even, deep[i], own)
            + side[3] * jnp.where(lane_row == RD - 1, above[i], spin(near[i], -2))
            + side[4] * jnp.where(lane_row == 0, below[i], spin(near[i], 2))
        )
    for h in range(2):
        for r, east_x, corner, north_y, south_y in (
            (-1, cb_s[2, halves(h), :], below, cb_s[1, halves(h), :], cb_s[0, halves(h), :]),
            (RD, cb_n[0, halves(h), :], above, cb_n[1, halves(h), :], cy_at(RD - 1, h)),
        ):
            around = spin(corner[1], -shift_of(max(0, min(r, RD - 1)), NF, h))
            west_x = jnp.where(first, around, spin(east_x, 1))
            keep_weights(r, h, weights(east_x, west_x, north_y, south_y))

    def complete(k):
        f0, f1 = CHUNKS[k]
        for h in range(2):
            low = [coef[i, 0, halves(h), :] for i in range(5)]
            high = [coef[i, RD + 1, halves(h), :] for i in range(5)]
            for f in range(f0, f1):
                at = halves(h, f)
                q1[0, at, :] = stencil(
                    low,
                    halo_s[1, at, :],
                    q0[0, at, :],
                    halo_s[0, at, :],
                    spin(below[f // 8], -shift_of(0, f, h)),
                )
                q1[RD + 1, at, :] = stencil(
                    high,
                    halo_n[0, at, :],
                    halo_n[1, at, :],
                    q0[RD - 1, at, :],
                    spin(above[f // 8], -shift_of(RD - 1, f, h)),
                )
        for h in range(2):
            for r in range(RD):
                c = [coef[i, r + 1, halves(h), :] for i in range(5)]
                for f in range(f0, f1):
                    at = halves(h, f)
                    adv[pl.ds(BASE[k] + (r * (f1 - f0) + f - f0) * LEV + h * 8, 8), :] = stencil(
                        c,
                        q1[r + 1, at, :],
                        q1[r + 2, at, :],
                        q1[r, at, :],
                        spin(beside[f // 8], -shift_of(r, f, h)),
                    )

    heat_rows = [zero] * RD

    def physics(k):
        sets = [q for q in range(len(SETS)) if SETS[q][0] == k]

        def at(q, l):
            return pl.ds(128 * q + l, 8, stride=LEV)

        begin = []
        for q in sets:
            low = [adv[at(q, l), :] for l in range(HALF)]
            high = [adv[at(q, LEV - 1 - l), :] for l in range(HALF)]
            begin.append([a + b for a, b in zip(low, high)] + [a - b for a, b in zip(low, high)])
        state = [list(b) for b in begin]
        for s in range(4):
            part = [[None] * LEV for q in sets]
            for l in range(HALF):
                for j, q in enumerate(sets):
                    for odd in range(2):
                        m = odd * HALF + l
                        own = l + (odd if l == HALF - 1 else 0)
                        v = state[j][m] * t_inv[q, own] + t_b[q, m]
                        if l:
                            v = v + t_c[q, own] * part[j][m - 1]
                        part[j][m] = v
            for l in range(HALF - 2, -1, -1):
                for j, q in enumerate(sets):
                    for odd in range(2):
                        m = odd * HALF + l
                        part[j][m] = part[j][m] + t_c[q, l] * part[j][m + 1]
            for j, q in enumerate(sets):
                if s:
                    keep = kinds[q] >= (1 if s == 1 else 2)
                    part[j] = [jnp.where(keep, a, b) for a, b in zip(part[j], state[j])]
                state[j] = part[j]
        for j, q in enumerate(sets):
            heat = zero
            for l in range(HALF):
                even_t = 0.5 * (state[j][l] - begin[j][l])
                odd_t = 0.5 * (state[j][HALF + l] - begin[j][HALF + l])
                low_t, high_t = even_t + odd_t, even_t - odd_t
                heat = heat + (low_t * low_t + high_t * high_t)
                ob[at(q, l), :] = adv[at(q, l), :] + low_t
                ob[at(q, LEV - 1 - l), :] = adv[at(q, LEV - 1 - l), :] + high_t
            each = CHUNKS[k][1] - CHUNKS[k][0]
            for r in range(8 * SETS[q][1] // each, min(RD, -(-8 * (SETS[q][1] + 1) // each))):
                heat_rows[r] = heat_rows[r] + jnp.where(row_of[q] == r, heat, 0.0)

    for k in range(NC):
        if k:
            own_step(k)
        complete(k)
        physics(k)

    heats = []
    for r in range(RD):
        heat = jnp.sum(heat_rows[r], axis=0, keepdims=True) * (1.0 / (NF * LEV))
        heats.append(jnp.broadcast_to(heat, (8, CD)))
    for t in range(n_wide // 8):
        hi, lo = zero, zero
        for r in range(RD):
            hi = hi + jnp.where(t_rows[r] == hib[t], heats[r], 0.0)
            lo = lo + jnp.where(t_rows[r] == lob[t], heats[r], 0.0)
        hi = jnp.broadcast_to(jnp.sum(hi, axis=1, keepdims=True), (8, CD))
        lo = jnp.broadcast_to(jnp.sum(lo, axis=1, keepdims=True), (8, CD))
        slots = jnp.where(lane == 2, hib[t], lob[t]) - ((t * 8 + sub) * CELLS).astype(F32)
        msg[t * 8 : t * 8 + 8, :] = jnp.where(lane == 0, hi, jnp.where(lane == 1, lo, slots))
    got[pl.ds(w, 1), :] = jnp.full((1, CD), -1.0, F32)

    rung(2, 0)

    def post(i, carry):
        m, dy = i // NY, i % NY
        dz = nz // 2 + (1 - 2 * (m % 2)) * ((m + 1) // 2)
        to = wide_at(dz, dy)
        pltpu.make_async_remote_copy(
            msg.at[pl.ds(to, 1)],
            got.at[pl.ds(w, 1)],
            msg_send,
            msg_recv,
            device_id={"wide": to},
            device_id_type=pl.DeviceIdType.MESH,
        ).start()
        return carry

    lax.fori_loop(0, n_wide - NY, post, 0)
    lax.fori_loop(n_wide - NY + 1, n_wide, post, 0)

    base = w * RD
    mine = zero
    wide_lane = lax.broadcasted_iota(jnp.int32, (CD, CD), 0)
    for r in range(RD):
        t_row = tgtb[r : r + 1, :]
        here = jnp.broadcast_to(t_row // CD - base, (8, CD))
        a = jnp.where((here == sub) & (sub < RD), heats[r], 0.0)
        b = jnp.where(jnp.broadcast_to(t_row % CD, (CD, CD)) == wide_lane, 1.0, 0.0)
        mine = mine + lax.dot_general(
            a, b, (((1,), (1,)), ((), ())), precision=HIGH, preferred_element_type=F32
        )

    mine_out[...] = mine
    for c in sends:
        c.wait_send()
    everyone = pl.ds(0, n_wide - 1)
    pltpu.make_async_copy(msg.at[everyone], got.at[everyone], msg_send).wait()
    pltpu.make_async_copy(msg.at[everyone], got.at[everyone], msg_recv).wait()
    got_out[...] = got[...]


def finish(n_wide, state, got, mine, out_hbm, span_hbm, spanb, out_sem, span_sem):
    copies = []
    for k, (f0, f1) in enumerate(CHUNKS):
        size = (f1 - f0) * LEV
        for r in range(RD):
            c = pltpu.make_async_copy(
                state.at[pl.ds(BASE[k] + r * size, size)],
                out_hbm.at[pl.ds(f0 * LEV, size), r],
                out_sem.at[k, r],
            )
            c.start()
            copies.append(c)
    lane = lax.broadcasted_iota(jnp.int32, (8, CD), 1)
    sub = lax.broadcasted_iota(jnp.int32, (8, CD), 0)
    rows = [jnp.zeros((8, CD), F32) for r in range(RD)]
    place = [(lane + r * CD).astype(F32) for r in range(RD)]
    for t in range(n_wide // 8):
        tile = got[t * 8 : t * 8 + 8, :]
        value = [jnp.broadcast_to(tile[:, i : i + 1], (8, CD)) for i in range(2)]
        slot = [jnp.broadcast_to(tile[:, i + 2 : i + 3], (8, CD)) for i in range(2)]
        for r in range(RD):
            for i in range(2):
                rows[r] = rows[r] + jnp.where(slot[i] == place[r], value[i], 0.0)
    total = mine[...]
    for r in range(RD):
        arrived = jnp.broadcast_to(jnp.sum(rows[r], axis=0, keepdims=True), (8, CD))
        total = total + jnp.where(sub == r, arrived, 0.0)
    spanb[...] = total[0:RD]
    c = pltpu.make_async_copy(spanb, span_hbm, span_sem)
    c.start()
    for d in copies:
        d.wait()
    c.wait()


def body(n_wide, n_narrow, tracers, courant_x, courant_y, physics_ref, class_coeffs, span_target, cloud_class):
    anyspace = pl.BlockSpec(memory_space=pl.ANY)
    inside = pl.BlockSpec(memory_space=pltpu.VMEM)
    dma, regular = pltpu.SemaphoreType.DMA, pltpu.SemaphoreType.REGULAR
    vm = lambda *shape: pltpu.VMEM(shape, F32)
    tiles = n_wide // 8
    state, got, mine = pl.pallas_call(
        functools.partial(kernel, n_wide, n_narrow),
        out_shape=(
            vm(128 * len(SETS), CD),
            vm(n_wide, CD),
            vm(8, CD),
        ),
        in_specs=[pl.BlockSpec(memory_space=pltpu.HBM)] * 7,
        out_specs=[inside] * 3,
        scratch_shapes=[
            vm(RD, NF * LEV, CD),
            vm(RD + 2, NF * LEV, CD),
            vm(128 * len(SETS), CD),
            vm(2 * RD, LEV, CD),
            vm(3, LEV, CD),
            vm(2, LEV, CD),
            vm(NF, LEV),
            vm(3, 2, NF),
            pltpu.VMEM((RD, CD), jnp.int32),
            pltpu.VMEM((RD, CD), jnp.int32),
            vm(2, NF * LEV, CD),
            vm(2, NF * LEV, CD),
            vm(4, 8, CD),
            vm(2, 4, 8, CD),
            vm(4, 2, 8, CD),
            vm(5, RD + 2, LEV, CD),
            vm(len(SETS), HALF + 1, 8, CD),
            vm(len(SETS), LEV, 8, CD),
            vm(len(SETS), HALF + 1, 8, CD),
            vm(tiles, 8, CD),
            vm(tiles, 8, CD),
            vm(n_wide, CD),
            vm(n_wide, CD),
            dma((NC, RD)),
            dma((12,)),
            dma((NC, 2)),
            dma((NC, 2)),
            dma((2,)),
            dma((2,)),
            dma((2,)),
            dma((2,)),
            dma((4,)),
            dma((4,)),
            dma,
            dma,
            regular((3,)),
            regular,
        ],
        compiler_params=pltpu.CompilerParams(
            collective_id=0, has_side_effects=True
        ),
        name="transport_physics",
    )(
        tracers.reshape(NF * LEV, RD, CD),
        courant_x,
        courant_y,
        physics_ref,
        jnp.transpose(class_coeffs, (1, 0, 2)),
        span_target,
        cloud_class,
    )
    out, span = pl.pallas_call(
        functools.partial(finish, n_wide),
        out_shape=(
            jax.ShapeDtypeStruct((NF * LEV, RD, CD), F32),
            jax.ShapeDtypeStruct((RD, CD), F32),
        ),
        in_specs=[inside] * 3,
        out_specs=(anyspace, anyspace),
        scratch_shapes=[vm(RD, CD), dma((NC, RD)), dma],
        compiler_params=pltpu.CompilerParams(vmem_limit_bytes=4 << 20),
        name="finish",
    )(state, got, mine)
    return out.reshape(NF, LEV, RD, CD), span


def solution(mesh):
    return jax.shard_map(
        functools.partial(body, mesh.shape["wide"], mesh.shape["narrow"]),
        mesh=mesh,
        in_specs=(
            P(None, None, "wide", "narrow"),
            P(None, "wide", "narrow"),
            P(None, "wide", "narrow"),
            P(),
            P(),
            P("wide", "narrow"),
            P("wide", "narrow"),
        ),
        out_specs=(P(None, None, "wide", "narrow"), P("wide", "narrow")),
        check_vma=False,
    )
```

```python
import functools

import jax
import jax.numpy as jnp
from jax import lax
from jax.experimental import pallas as pl
from jax.experimental.pallas import tpu as pltpu
from jax.sharding import PartitionSpec as P

F32 = jnp.float32
NF, LEV, RD, CD = 13, 16, 4, 128
CELLS = RD * CD
HALF = LEV // 2
CHUNKS = ((0, 4), (4, 8), (8, 11), (11, 13))
NC = len(CHUNKS)
SETS = tuple((k, s) for k, (f0, f1) in enumerate(CHUNKS) for s in range(-(-RD * (f1 - f0) // 8)))
BASE = tuple(128 * [q[0] for q in SETS].index(k) for k in range(NC))
CX_AT, CY_AT = (0, 2, 3, 7), (1, 4, 5, 6)
NY = 4
HIGH = lax.Precision.HIGHEST


def kernel(
    n_wide,
    n_narrow,
    x_hbm,
    cx_hbm,
    cy_hbm,
    ref_hbm,
    cc_hbm,
    tgt_hbm,
    cls_hbm,
    ob,
    got_out,
    mine_out,
    q0,
    q1,
    adv,
    cb,
    cb_s,
    cb_n,
    refb,
    ccb,
    tgtb,
    clsb,
    halo_n,
    halo_s,
    edge_tx,
    edge_rx,
    corner_rx,
    coef,
    t_inv,
    t_b,
    t_c,
    hib,
    lob,
    msg,
    got,
    in_sem,
    small_sem,
    row_send,
    row_recv,
    cb_send,
    cb_recv,
    edge_send,
    edge_recv,
    corner_send,
    corner_recv,
    msg_send,
    msg_recv,
    ladder_sem,
    side_sem,
):
    nz = n_wide // NY
    w = lax.axis_index("wide")
    n = lax.axis_index("narrow")
    z, y = w // NY, w % NY

    def wide_at(dz, dy):
        return ((z + dz + nz) % nz) * NY + (y + dy) % NY

    north, south = (w + 1) % n_wide, (w + n_wide - 1) % n_wide
    east, west = (n + 1) % n_narrow, (n + n_narrow - 1) % n_narrow
    ladder = nz == 16

    barrier = pltpu.get_barrier_semaphore()

    def hello(**at):
        pl.semaphore_signal(barrier, 1, device_id=at, device_id_type=pl.DeviceIdType.MESH)

    hello(wide=north)
    hello(wide=south)
    hello(narrow=east)
    hello(narrow=west)
    hellos = 4
    if ladder:
        for dy in (1, 2, 3):
            hello(wide=wide_at(0, dy))
        for dz in (1, -1, 2, -2):
            hello(wide=wide_at(dz, 0))
        hellos += 7
    else:
        for i in range(1, n_wide):
            hello(wide=(w + i) % n_wide)
        hellos += n_wide - 1

    def fields(f0, f1):
        return pl.ds(f0 * LEV, (f1 - f0) * LEV)

    small = []

    def load(src, dst):
        c = pltpu.make_async_copy(src, dst, small_sem.at[len(small)])
        c.start()
        small.append(c)

    for r in range(RD):
        load(cx_hbm.at[:, r], cb.at[CX_AT[r]])
    for r in range(RD):
        load(cy_hbm.at[:, r], cb.at[CY_AT[r]])
    loads = []
    for k, (f0, f1) in enumerate(CHUNKS):
        for r in range(RD):
            c = pltpu.make_async_copy(
                x_hbm.at[fields(f0, f1), r],
                q0.at[r, fields(f0, f1)],
                in_sem.at[k, r],
            )
            c.start()
            loads.append(c)
    load(tgt_hbm, tgtb)
    load(cls_hbm, clsb)
    load(ref_hbm, refb)
    load(cc_hbm, ccb)

    lane = lax.broadcasted_iota(jnp.int32, (8, CD), 1)
    sub = lax.broadcasted_iota(jnp.int32, (8, CD), 0)
    first, last = lane == 0, lane == CD - 1
    edge = first | last
    inner = (lane == 1) | (lane == CD - 2)
    lane_row = ((lane + 1) // 2) % RD
    even = lane % 2 == 0
    zero = jnp.zeros((8, CD), F32)
    for k, (f0, f1) in enumerate(CHUNKS):
        start, stop = BASE[k] + RD * (f1 - f0) * LEV, (BASE + (128 * len(SETS),))[k + 1]
        if stop > start:
            adv[start:stop, :] = jnp.zeros((stop - start, CD), F32)

    def spin(v, shift):
        shift %= CD
        return pltpu.roll(v, shift, 1) if shift else v

    def shift_of(r, f, h):
        return 2 * ((f % 8) * 8 + h * RD + r)

    def packed(v, r, f, h, which=None):
        return spin(jnp.where(edge if which is None else which, v, 0.0), shift_of(r, f, h))

    def halves(h, f=0):
        return pl.ds(f * LEV + h * 8, 8)

    for c in small[: 2 * RD]:
        c.wait()
    for c in loads:
        c.wait()

    def cx_at(r, h):
        return cb[CX_AT[r], halves(h), :]

    def cy_at(r, h):
        return cb[CY_AT[r], halves(h), :]

    ends_of = []
    for i in range(2):
        outer, second = [], []
        for r in range(RD):
            a, b = zero, zero
            for f in range(8 * i, min(8 * i + 8, NF)):
                for h in range(2):
                    v = q0[r, halves(h, f), :]
                    a = a + packed(v, r, f, h)
                    b = b + packed(v, r, f, h, inner)
            if i:
                for h in range(2):
                    a = a + packed(cx_at(r, h), r, NF, h)
                    b = b + packed(cx_at(r, h), r, NF, h, inner)
                    a = a + packed(cy_at(r, h), r, NF + 1, h)
            outer.append(a)
            second.append(b)
        edge_tx[i] = (outer[0] + outer[1]) + (outer[2] + outer[3])
        ends_of.append((outer[0], outer[RD - 1]))
        edge_tx[2 + i] = (second[0] + second[1]) + (second[2] + second[3])
    edge_tx[4] = (ends_of[0][0] + spin(ends_of[1][0], 2)) + (ends_of[0][1] + spin(ends_of[1][1], -2))
    for c in small[2 * RD :]:
        c.wait()

    pl.semaphore_wait(barrier, hellos)

    sends = []

    def send(src, dst, ssem, rsem, **at):
        c = pltpu.make_async_remote_copy(
            src, dst, ssem, rsem, device_id=at, device_id_type=pl.DeviceIdType.MESH
        )
        c.start()
        sends.append(c)
        return c

    if ladder:
        for dz in (1, -1):
            pl.semaphore_signal(
                ladder_sem.at[0],
                1,
                device_id={"wide": wide_at(dz, 0)},
                device_id_type=pl.DeviceIdType.MESH,
            )

    def rung(i, dz):
        if ladder:
            pl.semaphore_wait(ladder_sem.at[i], 2)
            if dz:
                for s in (dz, -dz):
                    pl.semaphore_signal(
                        ladder_sem.at[i + 1],
                        1,
                        device_id={"wide": wide_at(s, 0)},
                        device_id_type=pl.DeviceIdType.MESH,
                    )

    def tell(sem, **at):
        pl.semaphore_signal(sem, 1, device_id=at, device_id_type=pl.DeviceIdType.MESH)

    tell(side_sem, narrow=east)
    tell(side_sem, narrow=west)

    def send_rows(k):
        part = fields(*CHUNKS[k])
        up = send(
            q0.at[pl.ds(RD - 2, 2), part],
            halo_s.at[:, part],
            row_send.at[k, 0],
            row_recv.at[k, 0],
            wide=north,
        )
        down = send(
            q0.at[pl.ds(0, 2), part],
            halo_n.at[:, part],
            row_send.at[k, 1],
            row_recv.at[k, 1],
            wide=south,
        )
        return (up, down)

    faces = (
        send(cb.at[pl.ds(5, 3)], cb_s, cb_send.at[0], cb_recv.at[0], wide=north),
        send(cb.at[pl.ds(0, 2)], cb_n, cb_send.at[1], cb_recv.at[1], wide=south),
    )
    rows = [send_rows(0)]
    edges = (
        send(edge_tx.at[pl.ds(0, 4)], edge_rx.at[0], edge_send.at[0], edge_recv.at[0], narrow=east),
        send(edge_tx.at[pl.ds(0, 4)], edge_rx.at[1], edge_send.at[1], edge_recv.at[1], narrow=west),
    )
    pl.semaphore_wait(side_sem, 2)
    corners = []
    for i, (ns, ew) in enumerate(((north, east), (north, west), (south, east), (south, west))):
        corners.append(
            send(
                edge_tx.at[4],
                corner_rx.at[i],
                corner_send.at[i],
                corner_recv.at[i],
                wide=ns,
                narrow=ew,
            )
        )
    rows += [send_rows(k) for k in range(1, NC)]
    rung(0, 3)

    class_rows = [jnp.broadcast_to(clsb[r : r + 1, :], (8, CD)) for r in range(RD)]

    def pairs_of(k, s, shape):
        f0, f1 = CHUNKS[k]
        at = 8 * s + lax.broadcasted_iota(jnp.int32, shape, 0)
        return at // (f1 - f0), jnp.where(at < RD * (f1 - f0), f0 + at % (f1 - f0), -1)

    kinds, row_of = [], []
    for q, (k, s) in enumerate(SETS):
        f0, f1 = CHUNKS[k]
        row, _ = pairs_of(k, s, (8, CD))
        kind = class_rows[0]
        for r in range(1, RD):
            kind = jnp.where(row == r, class_rows[r], kind)
        kinds.append(kind)
        row_of.append(row)
        _, field = pairs_of(k, s, (8, NF))
        hit = field == lax.broadcasted_iota(jnp.int32, (8, NF), 1)

        def column(category, j, hit=hit):
            row = jnp.broadcast_to(ccb[category, j : j + 1, :], (8, NF))
            total = jnp.sum(jnp.where(hit, row, 0.0), axis=1, keepdims=True)
            return jnp.broadcast_to(total * (1.0, 0.5, 0.25)[category], (8, CD))

        d, rate = (
            jnp.where(kind == 2, column(2, j), jnp.where(kind == 1, column(1, j), column(0, j)))
            for j in range(2)
        )
        _, field = pairs_of(k, s, (8, LEV))
        refs = jnp.zeros((8, LEV), F32)
        for f in range(f0, f1):
            refs = jnp.where(field == f, jnp.broadcast_to(refb[f : f + 1, :], (8, LEV)), refs)
        middle = 1.0 + rate + 2.0 * d
        ratio = None
        for l in range(HALF):
            diagonal = middle if l else 1.0 + rate + d
            denominator = diagonal - d * ratio if l else diagonal
            level = [jnp.broadcast_to(refs[:, m : m + 1], (8, CD)) for m in (l, LEV - 1 - l)]
            even_ref, odd_ref = rate * (level[0] + level[1]), rate * (level[0] - level[1])
            if l < HALF - 1:
                inverse = 1.0 / denominator
                ratio = d * inverse
                t_inv[q, l] = inverse
                t_c[q, l] = ratio
                t_b[q, l] = even_ref * inverse
                t_b[q, HALF + l] = odd_ref * inverse
            else:
                even_inv, odd_inv = 1.0 / (denominator - d), 1.0 / (denominator + d)
                t_inv[q, l] = even_inv
                t_inv[q, l + 1] = odd_inv
                t_c[q, l] = d * even_inv
                t_c[q, l + 1] = d * odd_inv
                t_b[q, l] = even_ref * even_inv
                t_b[q, HALF + l] = odd_ref * odd_inv

    target_f = tgtb[...].astype(F32)
    t_rows = [jnp.broadcast_to(target_f[r : r + 1], (8, CD)) for r in range(RD)]
    o_rows = [jnp.broadcast_to(tgtb[r : r + 1, :] // CELLS, (8, CD)) for r in range(RD)]

    def ends(t, carry):
        d = t * 8 + sub
        hi = jnp.full((8, CD), -1.0, F32)
        lo = jnp.full((8, CD), 1e9, F32)
        for r in range(RD):
            hit = o_rows[r] == d
            hi = jnp.maximum(hi, jnp.where(hit, t_rows[r], -1.0))
            lo = jnp.minimum(lo, jnp.where(hit, t_rows[r], 1e9))
        hib[t] = jnp.broadcast_to(jnp.max(hi, axis=1, keepdims=True), (8, CD))
        lob[t] = jnp.broadcast_to(jnp.min(lo, axis=1, keepdims=True), (8, CD))
        return carry

    lax.fori_loop(0, n_wide // 8, ends, 0)

    def merged(from_west, from_east, by_west, by_east):
        return jnp.where(even, spin(from_west, by_west), spin(from_east, by_east))

    def weights(east_x, west_x, north_y, south_y):
        return (
            1.0
            - jnp.maximum(east_x, 0.0)
            + jnp.minimum(west_x, 0.0)
            - jnp.maximum(north_y, 0.0)
            + jnp.minimum(south_y, 0.0),
            -jnp.minimum(east_x, 0.0),
            jnp.maximum(west_x, 0.0),
            -jnp.minimum(north_y, 0.0),
            jnp.maximum(south_y, 0.0),
        )

    def keep_weights(r, h, values):
        for i, v in enumerate(values):
            coef[i, r + 1, halves(h), :] = v

    def stencil(c, here, north_q, south_q, around):
        east_q = jnp.where(last, around, spin(here, -1))
        west_q = jnp.where(first, around, spin(here, 1))
        return ((c[0] * here + c[3] * north_q) + c[4] * south_q) + (c[1] * east_q + c[2] * west_q)

    edges[0].wait_recv()
    edges[1].wait_recv()
    near = [merged(edge_rx[0, i], edge_rx[1, i], 1, -1) for i in range(2)]
    deep = [merged(edge_rx[0, 2 + i], edge_rx[1, 2 + i], 2, -2) for i in range(2)]
    faces[0].wait_recv()
    faces[1].wait_recv()
    for h in range(2):
        for r in range(RD):
            east_x = cx_at(r, h)
            around = spin(near[1], -shift_of(r, NF, h))
            west_x = jnp.where(first, around, spin(east_x, 1))
            south_y = cy_at(r - 1, h) if r else cb_s[1, halves(h), :]
            keep_weights(r, h, weights(east_x, west_x, cy_at(r, h), south_y))

    def own_step(k):
        f0, f1 = CHUNKS[k]
        for c in rows[k]:
            c.wait_recv()
        for h in range(2):
            for r in range(RD):
                c = [coef[i, r + 1, halves(h), :] for i in range(5)]
                for f in range(f0, f1):
                    at = halves(h, f)
                    q1[r + 1, at, :] = stencil(
                        c,
                        q0[r, at, :],
                        q0[r + 1, at, :] if r < RD - 1 else halo_n[0, at, :],
                        q0[r - 1, at, :] if r else halo_s[1, at, :],
                        spin(near[f // 8], -shift_of(r, f, h)),
                    )

    rung(1, 4)
    own_step(0)

    for c in corners:
        c.wait_recv()
    below = [merged(corner_rx[0], corner_rx[1], b, b - 2) for b in (-5, -3)]
    above = [merged(corner_rx[2], corner_rx[3], b, b - 2) for b in (7, 5)]
    cx_shift, cy_shift = -16 * (NF % 8), -16 * (NF % 8 + 1)
    side_y = spin(near[1], cy_shift)
    side = []
    for v in weights(
        spin(near[1], cx_shift),
        jnp.where(even, spin(deep[1], cx_shift), spin(edge_tx[1], cx_shift)),
        side_y,
        jnp.where(lane_row == 0, spin(below[1], cy_shift), spin(side_y, 2)),
    ):
        v = jnp.where((lane + 1) % CD < 16, v, 0.0)
        for by in (16, 32, 64):
            v = v + spin(v, by)
        side.append(v)
    beside = []
    for i in range(2):
        own = edge_tx[i]
        beside.append(
            side[0] * near[i]
            + side[1] * jnp.where(even, own, deep[i])
            + side[2] * jnp.where(even, deep[i], own)
            + side[3] * jnp.where(lane_row == RD - 1, above[i], spin(near[i], -2))
            + side[4] * jnp.where(lane_row == 0, below[i], spin(near[i], 2))
        )
    for h in range(2):
        for r, east_x, corner, north_y, south_y in (
            (-1, cb_s[2, halves(h), :], below, cb_s[1, halves(h), :], cb_s[0, halves(h), :]),
            (RD, cb_n[0, halves(h), :], above, cb_n[1, halves(h), :], cy_at(RD - 1, h)),
        ):
            around = spin(corner[1], -shift_of(max(0, min(r, RD - 1)), NF, h))
            west_x = jnp.where(first, around, spin(east_x, 1))
            keep_weights(r, h, weights(east_x, west_x, north_y, south_y))

    def complete(k):
        f0, f1 = CHUNKS[k]
        for h in range(2):
            low = [coef[i, 0, halves(h), :] for i in range(5)]
            high = [coef[i, RD + 1, halves(h), :] for i in range(5)]
            for f in range(f0, f1):
                at = halves(h, f)
                q1[0, at, :] = stencil(
                    low,
                    halo_s[1, at, :],
                    q0[0, at, :],
                    halo_s[0, at, :],
                    spin(below[f // 8], -shift_of(0, f, h)),
                )
                q1[RD + 1, at, :] = stencil(
                    high,
                    halo_n[0, at, :],
                    halo_n[1, at, :],
                    q0[RD - 1, at, :],
                    spin(above[f // 8], -shift_of(RD - 1, f, h)),
                )
        for h in range(2):
            for r in range(RD):
                c = [coef[i, r + 1, halves(h), :] for i in range(5)]
                for f in range(f0, f1):
                    at = halves(h, f)
                    adv[pl.ds(BASE[k] + (r * (f1 - f0) + f - f0) * LEV + h * 8, 8), :] = stencil(
                        c,
                        q1[r + 1, at, :],
                        q1[r + 2, at, :],
                        q1[r, at, :],
                        spin(beside[f // 8], -shift_of(r, f, h)),
                    )

    heat_rows = [zero] * RD

    def physics(k):
        sets = [q for q in range(len(SETS)) if SETS[q][0] == k]

        def at(q, l):
            return pl.ds(128 * q + l, 8, stride=LEV)

        begin = []
        for q in sets:
            low = [adv[at(q, l), :] for l in range(HALF)]
            high = [adv[at(q, LEV - 1 - l), :] for l in range(HALF)]
            begin.append([a + b for a, b in zip(low, high)] + [a - b for a, b in zip(low, high)])
        state = [list(b) for b in begin]
        for s in range(4):
            part = [[None] * LEV for q in sets]
            for l in range(HALF):
                for j, q in enumerate(sets):
                    for odd in range(2):
                        m = odd * HALF + l
                        own = l + (odd if l == HALF - 1 else 0)
                        v = state[j][m] * t_inv[q, own] + t_b[q, m]
                        if l:
                            v = v + t_c[q, own] * part[j][m - 1]
                        part[j][m] = v
            for l in range(HALF - 2, -1, -1):
                for j, q in enumerate(sets):
                    for odd in range(2):
                        m = odd * HALF + l
                        part[j][m] = part[j][m] + t_c[q, l] * part[j][m + 1]
            for j, q in enumerate(sets):
                if s:
                    keep = kinds[q] >= (1 if s == 1 else 2)
                    part[j] = [jnp.where(keep, a, b) for a, b in zip(part[j], state[j])]
                state[j] = part[j]
        for j, q in enumerate(sets):
            heat = zero
            for l in range(HALF):
                even_t = 0.5 * (state[j][l] - begin[j][l])
                odd_t = 0.5 * (state[j][HALF + l] - begin[j][HALF + l])
                low_t, high_t = even_t + odd_t, even_t - odd_t
                heat = heat + (low_t * low_t + high_t * high_t)
                ob[at(q, l), :] = adv[at(q, l), :] + low_t
                ob[at(q, LEV - 1 - l), :] = adv[at(q, LEV - 1 - l), :] + high_t
            each = CHUNKS[k][1] - CHUNKS[k][0]
            for r in range(8 * SETS[q][1] // each, min(RD, -(-8 * (SETS[q][1] + 1) // each))):
                heat_rows[r] = heat_rows[r] + jnp.where(row_of[q] == r, heat, 0.0)

    for k in range(NC):
        if k:
            own_step(k)
        complete(k)
        physics(k)

    heats = []
    for r in range(RD):
        heat = jnp.sum(heat_rows[r], axis=0, keepdims=True) * (1.0 / (NF * LEV))
        heats.append(jnp.broadcast_to(heat, (8, CD)))
    for t in range(n_wide // 8):
        hi, lo = zero, zero
        for r in range(RD):
            hi = hi + jnp.where(t_rows[r] == hib[t], heats[r], 0.0)
            lo = lo + jnp.where(t_rows[r] == lob[t], heats[r], 0.0)
        hi = jnp.broadcast_to(jnp.sum(hi, axis=1, keepdims=True), (8, CD))
        lo = jnp.broadcast_to(jnp.sum(lo, axis=1, keepdims=True), (8, CD))
        slots = jnp.where(lane == 2, hib[t], lob[t]) - ((t * 8 + sub) * CELLS).astype(F32)
        msg[t * 8 : t * 8 + 8, :] = jnp.where(lane == 0, hi, jnp.where(lane == 1, lo, slots))
    got[pl.ds(w, 1), :] = jnp.full((1, CD), -1.0, F32)

    rung(2, 0)

    def post(i, carry):
        m, dy = i // NY, i % NY
        dz = nz // 2 + (1 - 2 * (m % 2)) * ((m + 1) // 2)
        to = wide_at(dz, dy)
        pltpu.make_async_remote_copy(
            msg.at[pl.ds(to, 1)],
            got.at[pl.ds(w, 1)],
            msg_send,
            msg_recv,
            device_id={"wide": to},
            device_id_type=pl.DeviceIdType.MESH,
        ).start()
        return carry

    lax.fori_loop(0, n_wide - NY, post, 0)
    lax.fori_loop(n_wide - NY + 1, n_wide, post, 0)

    base = w * RD
    mine = zero
    wide_lane = lax.broadcasted_iota(jnp.int32, (CD, CD), 0)
    for r in range(RD):
        t_row = tgtb[r : r + 1, :]
        here = jnp.broadcast_to(t_row // CD - base, (8, CD))
        a = jnp.where((here == sub) & (sub < RD), heats[r], 0.0)
        b = jnp.where(jnp.broadcast_to(t_row % CD, (CD, CD)) == wide_lane, 1.0, 0.0)
        mine = mine + lax.dot_general(
            a, b, (((1,), (1,)), ((), ())), precision=HIGH, preferred_element_type=F32
        )

    mine_out[...] = mine
    for c in sends:
        c.wait_send()
    everyone = pl.ds(0, n_wide - 1)
    pltpu.make_async_copy(msg.at[everyone], got.at[everyone], msg_send).wait()
    pltpu.make_async_copy(msg.at[everyone], got.at[everyone], msg_recv).wait()
    got_out[...] = got[...]


def finish(n_wide, state, got, mine, out_hbm, span_hbm, spanb, out_sem, span_sem):
    copies = []
    for k, (f0, f1) in enumerate(CHUNKS):
        size = (f1 - f0) * LEV
        for r in range(RD):
            c = pltpu.make_async_copy(
                state.at[pl.ds(BASE[k] + r * size, size)],
                out_hbm.at[pl.ds(f0 * LEV, size), r],
                out_sem.at[k, r],
            )
            c.start()
            copies.append(c)
    lane = lax.broadcasted_iota(jnp.int32, (8, CD), 1)
    sub = lax.broadcasted_iota(jnp.int32, (8, CD), 0)
    rows = [jnp.zeros((8, CD), F32) for r in range(RD)]
    place = [(lane + r * CD).astype(F32) for r in range(RD)]
    for t in range(n_wide // 8):
        tile = got[t * 8 : t * 8 + 8, :]
        value = [jnp.broadcast_to(tile[:, i : i + 1], (8, CD)) for i in range(2)]
        slot = [jnp.broadcast_to(tile[:, i + 2 : i + 3], (8, CD)) for i in range(2)]
        for r in range(RD):
            for i in range(2):
                rows[r] = rows[r] + jnp.where(slot[i] == place[r], value[i], 0.0)
    total = mine[...]
    for r in range(RD):
        arrived = jnp.broadcast_to(jnp.sum(rows[r], axis=0, keepdims=True), (8, CD))
        total = total + jnp.where(sub == r, arrived, 0.0)
    spanb[...] = total[0:RD]
    c = pltpu.make_async_copy(spanb, span_hbm, span_sem)
    c.start()
    for d in copies:
        d.wait()
    c.wait()


def body(n_wide, n_narrow, tracers, courant_x, courant_y, physics_ref, class_coeffs, span_target, cloud_class):
    anyspace = pl.BlockSpec(memory_space=pl.ANY)
    inside = pl.BlockSpec(memory_space=pltpu.VMEM)
    dma, regular = pltpu.SemaphoreType.DMA, pltpu.SemaphoreType.REGULAR
    vm = lambda *shape: pltpu.VMEM(shape, F32)
    tiles = n_wide // 8
    state, got, mine = pl.pallas_call(
        functools.partial(kernel, n_wide, n_narrow),
        out_shape=(
            vm(128 * len(SETS), CD),
            vm(n_wide, CD),
            vm(8, CD),
        ),
        in_specs=[pl.BlockSpec(memory_space=pltpu.HBM)] * 7,
        out_specs=[inside] * 3,
        scratch_shapes=[
            vm(RD, NF * LEV, CD),
            vm(RD + 2, NF * LEV, CD),
            vm(128 * len(SETS), CD),
            vm(2 * RD, LEV, CD),
            vm(3, LEV, CD),
            vm(2, LEV, CD),
            vm(NF, LEV),
            vm(3, 2, NF),
            pltpu.VMEM((RD, CD), jnp.int32),
            pltpu.VMEM((RD, CD), jnp.int32),
            vm(2, NF * LEV, CD),
            vm(2, NF * LEV, CD),
            vm(5, 8, CD),
            vm(2, 4, 8, CD),
            vm(4, 8, CD),
            vm(5, RD + 2, LEV, CD),
            vm(len(SETS), HALF + 1, 8, CD),
            vm(len(SETS), LEV, 8, CD),
            vm(len(SETS), HALF + 1, 8, CD),
            vm(tiles, 8, CD),
            vm(tiles, 8, CD),
            vm(n_wide, CD),
            vm(n_wide, CD),
            dma((NC, RD)),
            dma((12,)),
            dma((NC, 2)),
            dma((NC, 2)),
            dma((2,)),
            dma((2,)),
            dma((2,)),
            dma((2,)),
            dma((4,)),
            dma((4,)),
            dma,
            dma,
            regular((3,)),
            regular,
        ],
        compiler_params=pltpu.CompilerParams(
            collective_id=0, has_side_effects=True
        ),
        name="transport_physics",
    )(
        tracers.reshape(NF * LEV, RD, CD),
        courant_x,
        courant_y,
        physics_ref,
        jnp.transpose(class_coeffs, (1, 0, 2)),
        span_target,
        cloud_class,
    )
    out, span = pl.pallas_call(
        functools.partial(finish, n_wide),
        out_shape=(
            jax.ShapeDtypeStruct((NF * LEV, RD, CD), F32),
            jax.ShapeDtypeStruct((RD, CD), F32),
        ),
        in_specs=[inside] * 3,
        out_specs=(anyspace, anyspace),
        scratch_shapes=[vm(RD, CD), dma((NC, RD)), dma],
        compiler_params=pltpu.CompilerParams(vmem_limit_bytes=4 << 20),
        name="finish",
    )(state, got, mine)
    return out.reshape(NF, LEV, RD, CD), span


def solution(mesh):
    return jax.shard_map(
        functools.partial(body, mesh.shape["wide"], mesh.shape["narrow"]),
        mesh=mesh,
        in_specs=(
            P(None, None, "wide", "narrow"),
            P(None, "wide", "narrow"),
            P(None, "wide", "narrow"),
            P(),
            P(),
            P("wide", "narrow"),
            P("wide", "narrow"),
        ),
        out_specs=(P(None, None, "wide", "narrow"), P("wide", "narrow")),
        check_vma=False,
    )
```
